128 devices in a mesh: ctx: 16 (over x, y_hi, core), tp: 8 (over y_lo, z).
Axes of the slice: x: 4, y: 4 (y_hi: 2, y_lo: 2; y = y_hi * 2 + y_lo), z: 4, core: 2. Of those that a mesh axis runs over, the one named last changes fastest.
Arguments:
- queries: bfloat16 [4096, 8192], P('ctx', 'tp'), may hold values from -120 to 120
- key_proj: bfloat16 [4096, 1024], P('ctx', 'tp'), may hold values from -4 to 4
- value_proj: bfloat16 [4096, 1024], P('ctx', 'tp'), may hold values from -6 to 6
- out_weight: bfloat16 [8192, 8192], P('tp'), may hold values from -0.75 to 0.75
- doc_ids: int32 [4096], replicated, may hold values from 0 to 7, never falling along the last dimension, each value on 1 to 2048 neighbouring positions
- drop_seed: int32 [1], replicated, may hold values from 0 to 1073741823
Outputs:
- output: bfloat16 [4096, 8192], P('ctx', 'tp')
The draws below stay inside these ranges and needn't reach their ends.
Inputs may be any that keep to these rules, and one draw needn't show every extreme that they name: doc_ids never fall along the sequence; each document has 1 to 2048 tokens, one exactly 2048.
All inputs are finite; a program needn't handle non-finite values.
Results may differ from the reference program's by a relative error of at most 0.019.
Values may be sent and summed in bfloat16 or wider, within the bound.
No kernel may reach another device: no remote copies, remote signals or barrier semaphores. Data moves between devices by JAX's collectives and lax.ppermute only.
A program may use at most 128 MiB of HBM per device.

```python
import math
import jax
import jax.numpy as jnp
import numpy as np
from jax import lax

D = 8192
HEADS = 64
KVH = 8
HD = 128
TOK_DEV = 256
DOCS = 8
SEQ = 4096


def shared_keys(key):
    drawn = jax.random.normal(jax.random.fold_in(key, 11), (SEQ, KVH * HD), jnp.float32)
    return jnp.clip(drawn, -4.0, 4.0)


def draw_key_proj(key, part):
    basis = shared_keys(key)
    return basis.astype(jnp.bfloat16)


def draw_queries(key, part):
    drawn = jax.random.normal(jax.random.fold_in(key, 13), (SEQ, HEADS * HD), jnp.float32)
    drawn = jnp.clip(drawn, -5.0, 5.0)
    return drawn.astype(jnp.bfloat16)


def block_scale(key, extent, cuts, low, largest):
    def one(axis_at, parts):
        steps = jax.random.uniform(jax.random.fold_in(jax.random.fold_in(key, 6), axis_at), (parts,), jnp.float32, low / len(cuts), largest / len(cuts))
        return jnp.repeat(jnp.exp(steps), extent[axis_at] // parts).reshape((-1,) + (1,) * (len(extent) - axis_at - 1))

    gain = one(*cuts[0])
    for cut in cuts[1:]:
        gain = gain * one(*cut)
    return gain


def length_profile(amount, total, bound, slope):
    weights = [(1 << 20) // math.isqrt(grade ** slope) + 1 for grade in range(2, amount + 1)]
    surplus, given = total - bound - (amount - 1), [1] * (amount - 1)
    while surplus > 0:
        movable = [i for i in range(amount - 1) if given[i] < bound]
        pool, left = sum([weights[i] for i in movable]), surplus
        for i in movable:
            extra = min(bound - given[i], max(1, left * weights[i] // pool), surplus)
            given[i] = given[i] + extra
            surplus = surplus - extra
    return np.array([bound] + given)


def ragged_sizes(key, number_of, total, most, lean):
    if number_of == 2:
        one = jax.random.randint(key, (), max(1, total - most), min(most, total - 1) + 1)
        return jnp.stack([one, total - one])
    tallies = jnp.asarray(length_profile(number_of, total, most, lean), jnp.int32)
    twos = (number_of - 1) // 2
    donor, receiver = tallies[1:1 + 2 * twos:2], tallies[2:2 + 2 * twos:2]
    room = jnp.minimum(donor - 1, most - receiver)
    shifted = jax.random.randint(jax.random.fold_in(key, 1), (twos,), 0, 1 << 20) % (room + 1)
    tallies = tallies.at[1:1 + 2 * twos:2].set(donor - shifted).at[2:2 + 2 * twos:2].set(receiver + shifted)
    return tallies[jax.random.permutation(jax.random.fold_in(key, 2), number_of)]


def gaussian(stream_key, dims, deviation, reach, pieces=(), kind=jnp.bfloat16):
    values = jax.random.normal(stream_key, dims, jnp.float32) * deviation
    if len(pieces) > 0:
        values = block_scale(stream_key, dims, pieces, -0.22, 0.18) * values
    return jnp.clip(values, min=-reach, max=reach).astype(kind)


def setup_inputs(seed: int = 0) -> dict:
    key_of = jax.random.split(jax.random.key(seed), 7)
    queries = draw_queries(jax.random.fold_in(key_of[6], 71), 0)
    key_proj = draw_key_proj(jax.random.fold_in(key_of[6], 71), 0)
    value_proj = gaussian(key_of[2], (SEQ, KVH * HD), 1.0, 6.0, ((0, 16), (1, 8)))
    out_weight = gaussian(key_of[3], (HEADS * HD, D), 64 ** -0.5, 0.75, ((0, 8),))
    doc_ids = jnp.searchsorted(jnp.cumsum(ragged_sizes(key_of[4], DOCS, SEQ, SEQ // 2, 0)), jnp.arange(SEQ), side="right").astype(jnp.int32)
    drop_seed = jax.random.randint(key_of[5], (1,), 0, 1073741824).astype(jnp.int32)
    return dict(queries=queries, key_proj=key_proj, value_proj=value_proj, out_weight=out_weight, doc_ids=doc_ids, drop_seed=drop_seed)


def mixing(value):
    value = value ^ lax.shift_right_logical(value, jnp.int32(16))
    value = value * 73244475
    value = value ^ lax.shift_right_logical(value, jnp.int32(16))
    value = value * 73244475
    value = value ^ lax.shift_right_logical(value, jnp.int32(16))
    return value


def reference(queries, key_proj, value_proj, out_weight, doc_ids, drop_seed):
    per_group = HEADS // KVH
    blocks = SEQ // TOK_DEV
    positions = jnp.arange(SEQ, dtype=jnp.int32)
    factor = HD ** -0.5

    def one_block(index):
        block = index // KVH
        group = index % KVH
        start = (block * TOK_DEV).astype(jnp.int32)
        column = (group * per_group * HD).astype(jnp.int32)
        q_rows = lax.dynamic_slice(queries, (start, column), (TOK_DEV, per_group * HD))
        q_rows = q_rows.reshape(TOK_DEV, per_group, HD).astype(jnp.float32)
        k_cols = lax.dynamic_slice_in_dim(key_proj, (group * HD).astype(jnp.int32), HD, 1).astype(jnp.float32)
        v_cols = lax.dynamic_slice_in_dim(value_proj, (group * HD).astype(jnp.int32), HD, 1).astype(jnp.float32)
        scores = jnp.einsum("qgd,nd->qgn", q_rows, k_cols) * factor
        q_pos = start + jnp.arange(TOK_DEV, dtype=jnp.int32)
        q_doc = lax.dynamic_slice_in_dim(doc_ids, start, TOK_DEV)
        allowed = (q_doc[:, None] == doc_ids[None, :]) & (positions[None, :] <= q_pos[:, None])
        allowed = allowed[:, None, :]
        peak = jnp.max(jnp.where(allowed, scores, jnp.float32(-1e30)), axis=-1)
        weights = jnp.where(allowed, jnp.exp(scores - peak[..., None]), jnp.float32(0.0))
        row_sum = jnp.sum(weights, axis=-1)
        head_ids = (group * per_group + jnp.arange(per_group, dtype=jnp.int32)).reshape(1, per_group, 1)
        q_hash = mixing(mixing(drop_seed[0] * 7919 + head_ids) ^ (q_pos.reshape(TOK_DEV, 1, 1) * 65537))
        full_hash = mixing(q_hash + positions.reshape(1, 1, SEQ))
        keeper = lax.shift_right_logical(full_hash, jnp.int32(8)) >= 1677722
        dropped = jnp.where(keeper, weights * jnp.float32(1.0 / 0.9), jnp.float32(0.0)).astype(jnp.bfloat16)
        mixed = jnp.einsum("qgn,nd->qgd", dropped.astype(jnp.float32), v_cols) / row_sum[..., None]
        return mixed.astype(jnp.bfloat16)

    results = lax.map(one_block, jnp.arange(blocks * KVH, dtype=jnp.int32))
    attention = results.reshape(blocks, KVH, TOK_DEV, per_group, HD)
    attention = attention.transpose(0, 2, 1, 3, 4).reshape(SEQ, HEADS * HD)
    return jnp.dot(attention, out_weight, preferred_element_type=jnp.float32).astype(jnp.bfloat16)
```

```python
import functools
import math

import jax
import jax.numpy as jnp
from jax import lax
from jax.experimental import pallas as pl
from jax.experimental.pallas import tpu as pltpu
from jax.sharding import PartitionSpec as P

HEADS = 64
KVH = 8
HD = 128
GROUP = HEADS // KVH
ROWS = 256
BACK = 8
QUERY_SCALE = HD ** (-0.5) * math.log2(math.e)
INT_MIN = -(1 << 31)
KEEP_FLIP = 0x1999 + INT_MIN
KEEP_BOUND = (1677722 << 8) + INT_MIN
COLUMNS = 1024
SET_COLUMNS = ((0, 384), (384, 768), (768, 1024))
LINK_FLIPS = (1, 3, 4)
SET_LINKS = ((0, 1, 2), (1, 2, 0), (2, 0, 1))
MIB = 1 << 20


def xor_shift(value):
    return value ^ lax.shift_right_logical(value, jnp.int32(16))


def mixing(value):
    value = xor_shift(value) * 73244475
    value = xor_shift(value) * 73244475
    return xor_shift(value)


def keep_body(table, keep_hbm, keep, row_hash, sems):
    n = table[0]
    row0 = table[1]
    head0 = table[2]
    seed = table[3]
    rows = row0 + lax.broadcasted_iota(jnp.int32, (ROWS, 128), 0)
    lanes = lax.broadcasted_iota(jnp.int32, (ROWS, 128), 1)
    for h in range(GROUP):
        head_hash = mixing(jnp.full((ROWS, 128), seed * 7919 + head0 + h, jnp.int32))
        row_hash[h] = mixing(head_hash ^ (rows * 65537)) + lanes

    def block(d, _):
        start = row0 - d * ROWS

        def head(h, _):
            for half in range(2):
                value = row_hash[h] + (start + half * 128)
                value = xor_shift(value) * 73244475
                value = xor_shift(value) * 73244475
                kept = (value ^ KEEP_FLIP) >= KEEP_BOUND
                keep[d, h, :, half * 128 : (half + 1) * 128] = jnp.where(
                    kept, jnp.float32(1), jnp.float32(0)
                ).astype(jnp.bfloat16)
            return 0

        lax.fori_loop(0, GROUP, head, 0)
        pltpu.make_async_copy(keep.at[d], keep_hbm.at[d], sems.at[d]).start()
        return 0

    lax.fori_loop(0, n + 1, block, 0)

    def finish(d, _):
        pltpu.make_async_copy(keep.at[d], keep_hbm.at[d], sems.at[d]).wait()
        return 0

    lax.fori_loop(0, n + 1, finish, 0)


def keep_masks(table):
    return pl.pallas_call(
        keep_body,
        out_shape=jax.ShapeDtypeStruct((BACK + 1, GROUP, ROWS, ROWS), jnp.bfloat16),
        in_specs=[pl.BlockSpec(memory_space=pltpu.SMEM)],
        out_specs=pl.BlockSpec(memory_space=pl.ANY),
        scratch_shapes=[
            pltpu.VMEM((BACK + 1, GROUP, ROWS, ROWS), jnp.bfloat16),
            pltpu.VMEM((GROUP, ROWS, 128), jnp.int32),
            pltpu.SemaphoreType.DMA((BACK + 1,)),
        ],
        compiler_params=pltpu.CompilerParams(vmem_limit_bytes=16 * MIB),
        cost_estimate=pl.CostEstimate(flops=400_000_000, bytes_accessed=10 * MIB, transcendentals=0),
        name="keep_masks",
    )(table)


def slot_flip(slot):
    return (slot & 1) ^ (3 * ((slot >> 1) & 1)) ^ (4 * (slot >> 2))


def attend_body(
    part,
    rows,
    table,
    low_ref,
    q_ref,
    own_hbm,
    other_hbm,
    keep_hbm,
    w_hbm,
    *refs,
):
    outs = refs[:6]
    kv, keep, weight, query, score, peak, total, accum, mixed, bias, kv_sem, keep_sem, w_sem = refs[6:]
    n = table[0]
    row0 = table[1] + part * rows
    shard = table[4]
    core = table[5]

    own_copy = pltpu.make_async_copy(own_hbm, kv.at[0], kv_sem.at[0])
    other_copy = pltpu.make_async_copy(other_hbm, kv.at[1], kv_sem.at[1])
    own_copy.start()
    other_copy.start()

    def keep_copy(d):
        return pltpu.make_async_copy(
            keep_hbm.at[d, :, pl.ds(part * rows, rows), :], keep.at[d], keep_sem.at[d]
        )

    def start_keep(d, _):
        keep_copy(d).start()
        return 0

    lax.fori_loop(0, n + 1, start_keep, 0)

    def w_copy(slot):
        column = pl.multiple_of((shard ^ slot_flip(slot)) * COLUMNS, COLUMNS)
        return pltpu.make_async_copy(
            w_hbm.at[:, pl.ds(column, COLUMNS)], weight.at[slot], w_sem.at[slot]
        )

    for slot in range(8):
        w_copy(slot).start()

    for h in range(GROUP):
        scaled = q_ref[:, h * HD : (h + 1) * HD].astype(jnp.float32) * QUERY_SCALE
        high = scaled.astype(jnp.bfloat16)
        query[h, :, :HD] = high
        query[h, :, HD:] = (scaled - high.astype(jnp.float32)).astype(jnp.bfloat16)
    peak[...] = jnp.full(peak.shape, -3e38, jnp.float32)
    total[...] = jnp.zeros(total.shape, jnp.float32)
    accum[...] = jnp.zeros(accum.shape, jnp.float32)
    own_copy.wait()
    other_copy.wait()

    def place(d):
        odd = d & 1
        return odd, jnp.where(odd == 1, (d + 1 - 2 * core) >> 1, d >> 1)

    last_low = low_ref[rows - 1, 0]

    def score_step(d, masked):
        side, at = place(d)
        keys = kv[side, at, :, :HD]
        keys = jnp.concatenate([keys, keys], axis=1)
        if masked:
            key_pos = (table[1] - d * ROWS) + lax.broadcasted_iota(jnp.int32, (rows, ROWS), 1)
            row_pos = row0 + lax.broadcasted_iota(jnp.int32, (rows, ROWS), 0)
            allowed = (key_pos >= low_ref[...]) & (key_pos <= row_pos)
            bias[...] = jnp.where(allowed, jnp.float32(0), jnp.float32(-1e30))
        for h in range(GROUP):
            value = lax.dot_general(
                query[h], keys, (((1,), (1,)), ((), ())), preferred_element_type=jnp.float32
            )
            if masked:
                value = value + bias[...]
            score[d, h] = value
            peak[h] = jnp.maximum(peak[h], jnp.maximum(value[:, :128], value[:, 128:]))

    def score_loop(d, _):
        free = (d > 0) & (table[1] - d * ROWS >= last_low)

        @pl.when(free)
        def _():
            score_step(d, False)

        @pl.when(jnp.logical_not(free))
        def _():
            score_step(d, True)

        return 0

    lax.fori_loop(0, n + 1, score_loop, 0)
    for h in range(GROUP):
        peak[h] = jnp.broadcast_to(jnp.max(peak[h], axis=1, keepdims=True), (rows, 128))

    def value_loop(d, _):
        side, at = place(d)
        values = kv[side, at, :, HD:]
        keep_copy(d).wait()
        for h in range(GROUP):
            top = peak[h]
            first = jnp.exp2(score[d, h, :, :128] - top)
            second = jnp.exp2(score[d, h, :, 128:] - top)
            total[h] = total[h] + (first + second)
            prob = jnp.concatenate([first.astype(jnp.bfloat16), second.astype(jnp.bfloat16)], axis=1)
            prob = prob * keep[d, h]
            accum[h] = accum[h] + jnp.dot(prob, values, preferred_element_type=jnp.float32)
        return 0

    lax.fori_loop(0, n + 1, value_loop, 0)
    for h in range(GROUP):
        row_sum = jnp.sum(total[h], axis=1, keepdims=True) * 0.9
        mixed[:, h * HD : (h + 1) * HD] = (accum[h] / row_sum).astype(jnp.bfloat16)

    for slot in range(8):
        w_copy(slot).wait()
        product = jnp.dot(mixed[...], weight[slot], preferred_element_type=jnp.float32)
        product = product.astype(jnp.bfloat16)
        bits = [(slot >> k) & 1 for k in range(3)]
        for s, (lo, hi) in enumerate(SET_COLUMNS):
            one, two, three = (bits[k] for k in SET_LINKS[s])
            outs[2 * s + one][2 * two + three] = product[:, lo:hi]


def attend(part, rows, table, low, queries, own, other, keep, weight):
    out_shape, out_specs = [], []
    for lo, hi in SET_COLUMNS:
        for _ in range(2):
            out_shape.append(jax.ShapeDtypeStruct((4, rows, hi - lo), jnp.bfloat16))
            out_specs.append(pl.BlockSpec((4, rows, hi - lo), lambda i: (0, 0, 0)))
    any_spec = pl.BlockSpec(memory_space=pl.ANY)
    outs = pl.pallas_call(
        functools.partial(attend_body, part, rows),
        out_shape=out_shape,
        grid=(1,),
        in_specs=[
            pl.BlockSpec(memory_space=pltpu.SMEM),
            pl.BlockSpec((rows, 1), lambda i: (part, 0)),
            pl.BlockSpec((rows, GROUP * HD), lambda i: (part, 0)),
            any_spec,
            any_spec,
            any_spec,
            any_spec,
        ],
        out_specs=out_specs,
        scratch_shapes=[
            pltpu.VMEM((2, 5, ROWS, 2 * HD), jnp.bfloat16),
            pltpu.VMEM((BACK + 1, GROUP, rows, ROWS), jnp.bfloat16),
            pltpu.VMEM((8, GROUP * HD, COLUMNS), jnp.bfloat16),
            pltpu.VMEM((GROUP, rows, 2 * HD), jnp.bfloat16),
            pltpu.VMEM((BACK + 1, GROUP, rows, ROWS), jnp.float32),
            pltpu.VMEM((GROUP, rows, 128), jnp.float32),
            pltpu.VMEM((GROUP, rows, 128), jnp.float32),
            pltpu.VMEM((GROUP, rows, HD), jnp.float32),
            pltpu.VMEM((rows, GROUP * HD), jnp.bfloat16),
            pltpu.VMEM((rows, ROWS), jnp.float32),
            pltpu.SemaphoreType.DMA((2,)),
            pltpu.SemaphoreType.DMA((BACK + 1,)),
            pltpu.SemaphoreType.DMA((8,)),
        ],
        compiler_params=pltpu.CompilerParams(vmem_limit_bytes=48 * MIB),
        cost_estimate=pl.CostEstimate(
            flops=3_000_000_000, bytes_accessed=24 * MIB, transcendentals=3_000_000
        ),
        name=f"attend_{part}",
    )(table, low, queries, own, other, keep, weight)
    return outs


def swap(array, flip):
    return lax.ppermute(array, "tp", [(i, i ^ flip) for i in range(8)])


def scatter_sums(outs):
    pieces = []
    for s in range(3):
        keep, send = outs[2 * s], outs[2 * s + 1]
        for step, link in enumerate(SET_LINKS[s]):
            got = swap(send, LINK_FLIPS[link])
            held = (keep.astype(jnp.float32) + got.astype(jnp.float32)).astype(jnp.bfloat16)
            half = held.shape[0] // 2
            keep, send = held[:half], held[half:]
        pieces.append(held[0])
    return jnp.concatenate(pieces, axis=1)


def body(queries, key_proj, value_proj, out_weight, doc_ids, drop_seed):
    ctx = lax.axis_index("ctx")
    tp = lax.axis_index("tp")
    row0 = ctx * ROWS
    q_doc = lax.dynamic_slice_in_dim(doc_ids, row0, ROWS)
    low = jnp.sum((doc_ids[None, :] < q_doc[:, None]).astype(jnp.int32), axis=1)
    n = ctx - low[0] // ROWS
    table = jnp.stack([n, row0, tp * GROUP, drop_seed[0], tp, ctx % 2]).astype(jnp.int32)

    own = jnp.concatenate([key_proj, value_proj], axis=1)
    column = [own]
    for chips in range(1, 5):
        pairs = [(i, (i + 2 * chips) % 16) for i in range(16)]
        column.append(lax.ppermute(own, "ctx", pairs))
    column = jnp.stack(column)
    other = lax.ppermute(column, "ctx", [(i, i ^ 1) for i in range(16)])

    keep = keep_masks(table)
    low = low.reshape(ROWS, 1)
    result = []
    rows = ROWS // 2
    for part in range(2):
        outs = attend(part, rows, table, low, queries, column, other, keep, out_weight)
        result.append(scatter_sums(outs))
    return jnp.concatenate(result, axis=0)


def solution(mesh):
    in_specs = (P("ctx", "tp"), P("ctx", "tp"), P("ctx", "tp"), P("tp", None), P(), P())
    return jax.shard_map(
        body, mesh=mesh, in_specs=in_specs, out_specs=P("ctx", "tp"), check_vma=False
    )
```

```python
import functools
import math

import jax
import jax.numpy as jnp
from jax import lax
from jax.experimental import pallas as pl
from jax.experimental.pallas import tpu as pltpu
from jax.sharding import PartitionSpec as P

HEADS = 64
KVH = 8
HD = 128
GROUP = HEADS // KVH
ROWS = 256
BACK = 8
QUERY_SCALE = HD ** (-0.5) * math.log2(math.e)
INT_MIN = -(1 << 31)
KEEP_FLIP = 0x1999 + INT_MIN
KEEP_BOUND = (1677722 << 8) + INT_MIN
COLUMNS = 1024
SET_COLUMNS = (((0, 384), (384, 768), (768, 1024)), ((0, 384), (384, 640), (640, 1024)))
LINK_FLIPS = (1, 3, 4)
SET_LINKS = ((0, 1, 2), (1, 2, 0), (2, 0, 1))
MIB = 1 << 20


def xor_shift(value):
    return value ^ lax.shift_right_logical(value, jnp.int32(16))


def mixing(value):
    value = xor_shift(value) * 73244475
    value = xor_shift(value) * 73244475
    return xor_shift(value)


def pack_body(k_hbm, v_hbm, out, sems):
    copies = [
        pltpu.make_async_copy(source, out.at[i], sems.at[i]) for i, source in enumerate((k_hbm, v_hbm))
    ]
    for copy in copies:
        copy.start()
    for copy in copies:
        copy.wait()


def pack(k, v):
    return pl.pallas_call(
        pack_body,
        out_shape=jax.ShapeDtypeStruct((2, ROWS, HD), jnp.bfloat16),
        in_specs=[pl.BlockSpec(memory_space=pl.ANY)] * 2,
        out_specs=pl.BlockSpec(memory_space=pltpu.VMEM),
        scratch_shapes=[pltpu.SemaphoreType.DMA((2,))],
        compiler_params=pltpu.CompilerParams(vmem_limit_bytes=1 * MIB),
        name="pack",
    )(k, v)


def row_low(starts, row):
    low = jnp.zeros_like(row)
    for v in range(1, 8):
        low = jnp.maximum(low, jnp.where(row >= starts[v], starts[v], 0))
    return low


def keep_body(seed_ref, docs, keep, starts, row_hash):
    row0 = lax.axis_index("ctx") * ROWS
    head0 = lax.axis_index("tp") * GROUP
    seed = seed_ref[0]
    starts[0] = 0
    for v in range(1, 8):
        starts[v] = jnp.sum((docs[...] < v).astype(jnp.int32))
    n = (row0 - (row_low(starts, row0) & -ROWS)) // ROWS
    rows = row0 + lax.broadcasted_iota(jnp.int32, (ROWS, 128), 0)
    lanes = lax.broadcasted_iota(jnp.int32, (ROWS, 128), 1)
    for h in range(GROUP):
        head_hash = mixing(jnp.full((8, 128), seed * 7919 + head0 + h, jnp.int32))[:1]
        row_hash[h] = mixing(head_hash ^ (rows * 65537)) + lanes

    def block(d, _):
        start = row0 - d * ROWS

        def head(h, _):
            for half in range(2):
                value = row_hash[h] + (start + half * 128)
                value = xor_shift(value) * 73244475
                value = xor_shift(value) * 73244475
                kept = (value ^ KEEP_FLIP) >= KEEP_BOUND
                keep[d, h, :, half * 128 : (half + 1) * 128] = jnp.where(
                    kept, jnp.float32(1), jnp.float32(0)
                ).astype(jnp.bfloat16)
            return 0

        lax.fori_loop(0, GROUP, head, 0)
        return 0

    lax.fori_loop(0, n + 1, block, 0)


def keep_masks(seed, docs):
    return pl.pallas_call(
        keep_body,
        out_shape=[
            jax.ShapeDtypeStruct((BACK + 1, GROUP, ROWS, ROWS), jnp.bfloat16),
            jax.ShapeDtypeStruct((8,), jnp.int32),
        ],
        in_specs=[
            pl.BlockSpec(memory_space=pltpu.SMEM),
            pl.BlockSpec(memory_space=pltpu.VMEM),
        ],
        out_specs=[
            pl.BlockSpec(memory_space=pltpu.VMEM),
            pl.BlockSpec(memory_space=pltpu.SMEM),
        ],
        scratch_shapes=[pltpu.VMEM((GROUP, ROWS, 128), jnp.int32)],
        compiler_params=pltpu.CompilerParams(vmem_limit_bytes=12 * MIB),
        cost_estimate=pl.CostEstimate(flops=400_000_000, bytes_accessed=10 * MIB, transcendentals=0),
        name="keep_masks",
    )(seed, docs)


def slot_flip(slot):
    return (slot & 1) ^ (3 * ((slot >> 1) & 1)) ^ (4 * (slot >> 2))


def attend_body(
    part,
    rows,
    starts,
    q_ref,
    own,
    other,
    keep,
    w_hbm,
    *refs,
):
    outs = refs[:6]
    kv, weight, query, score, peak, total, accum, mixed, bias, w_sem = refs[6:]
    ctx = lax.axis_index("ctx")
    block0 = ctx * ROWS
    row0 = block0 + part * rows
    shard = lax.axis_index("tp")
    core = ctx & 1
    n = (block0 - (row_low(starts, block0) & -ROWS)) // ROWS

    def w_copy(slot):
        column = pl.multiple_of((shard ^ slot_flip(slot)) * COLUMNS, COLUMNS)
        return pltpu.make_async_copy(
            w_hbm.at[:, pl.ds(column, COLUMNS)], weight.at[slot], w_sem.at[slot]
        )

    for slot in range(8):
        w_copy(slot).start()

    for h in range(GROUP):
        scaled = q_ref[:, h * HD : (h + 1) * HD].astype(jnp.float32) * QUERY_SCALE
        high = scaled.astype(jnp.bfloat16)
        query[h, :, :HD] = high
        query[h, :, HD:] = (scaled - high.astype(jnp.float32)).astype(jnp.bfloat16)
    peak[...] = jnp.full(peak.shape, -3e38, jnp.float32)
    total[...] = jnp.zeros(total.shape, jnp.float32)
    accum[...] = jnp.zeros(accum.shape, jnp.float32)

    for k in range(5):
        kv[0, k] = own[k]
        kv[1, k] = other[k]

    def place(d):
        odd = d & 1
        return odd, jnp.where(odd == 1, (d + 1 - 2 * core) >> 1, d >> 1)

    last_low = row_low(starts, row0 + rows - 1)

    def score_step(d, masked):
        side, at = place(d)
        keys = kv[side, at, 0]
        keys = jnp.concatenate([keys, keys], axis=1)
        if masked:
            key_pos = (block0 - d * ROWS) + lax.broadcasted_iota(jnp.int32, (rows, ROWS), 1)
            row_pos = row0 + lax.broadcasted_iota(jnp.int32, (rows, 1), 0)
            allowed = (key_pos >= row_low(starts, row_pos)) & (key_pos <= row_pos)
            bias[...] = jnp.where(allowed, jnp.float32(0), jnp.float32(-1e30))
        for h in range(GROUP):
            value = lax.dot_general(
                query[h], keys, (((1,), (1,)), ((), ())), preferred_element_type=jnp.float32
            )
            if masked:
                value = value + bias[...]
            score[d, h] = value
            peak[h] = jnp.maximum(peak[h], jnp.maximum(value[:, :128], value[:, 128:]))

    def score_loop(d, _):
        free = (d > 0) & (block0 - d * ROWS >= last_low)

        @pl.when(free)
        def _():
            score_step(d, False)

        @pl.when(jnp.logical_not(free))
        def _():
            score_step(d, True)

        return 0

    lax.fori_loop(0, n + 1, score_loop, 0)
    for h in range(GROUP):
        peak[h] = jnp.broadcast_to(jnp.max(peak[h], axis=1, keepdims=True), (rows, 128))

    def value_loop(d, _):
        side, at = place(d)
        values = kv[side, at, 1]
        for h in range(GROUP):
            top = peak[h]
            first = jnp.exp2(score[d, h, :, :128] - top)
            second = jnp.exp2(score[d, h, :, 128:] - top)
            total[h] = total[h] + (first + second)
            prob = jnp.concatenate([first.astype(jnp.bfloat16), second.astype(jnp.bfloat16)], axis=1)
            prob = prob * keep[d, h, pl.ds(part * rows, rows), :]
            accum[h] = accum[h] + jnp.dot(prob, values, preferred_element_type=jnp.float32)
        return 0

    lax.fori_loop(0, n + 1, value_loop, 0)
    for h in range(GROUP):
        row_sum = jnp.sum(total[h], axis=1, keepdims=True) * 0.9
        mixed[:, h * HD : (h + 1) * HD] = (accum[h] / row_sum).astype(jnp.bfloat16)

    for slot in range(8):
        w_copy(slot).wait()
        product = jnp.dot(mixed[...], weight[slot], preferred_element_type=jnp.float32)
        product = product.astype(jnp.bfloat16)
        bits = [(slot >> k) & 1 for k in range(3)]
        for s, (lo, hi) in enumerate(SET_COLUMNS[part]):
            one, two, three = (bits[k] for k in SET_LINKS[s])
            outs[2 * s + one][2 * two + three] = product[:, lo:hi]


def attend(part, rows, starts, queries, own, other, keep, weight):
    out_shape, out_specs = [], []
    for lo, hi in SET_COLUMNS[part]:
        for _ in range(2):
            out_shape.append(jax.ShapeDtypeStruct((4, rows, hi - lo), jnp.bfloat16))
            out_specs.append(pl.BlockSpec((4, rows, hi - lo), lambda i: (0, 0, 0)))
    vmem_spec = pl.BlockSpec(memory_space=pltpu.VMEM)
    outs = pl.pallas_call(
        functools.partial(attend_body, part, rows),
        out_shape=out_shape,
        grid=(1,),
        in_specs=[
            pl.BlockSpec(memory_space=pltpu.SMEM),
            pl.BlockSpec((rows, GROUP * HD), lambda i: (part, 0)),
            vmem_spec,
            vmem_spec,
            vmem_spec,
            pl.BlockSpec(memory_space=pl.ANY),
        ],
        out_specs=out_specs,
        scratch_shapes=[
            pltpu.VMEM((2, 5, 2, ROWS, HD), jnp.bfloat16),
            pltpu.VMEM((8, GROUP * HD, COLUMNS), jnp.bfloat16),
            pltpu.VMEM((GROUP, rows, 2 * HD), jnp.bfloat16),
            pltpu.VMEM((BACK + 1, GROUP, rows, ROWS), jnp.float32),
            pltpu.VMEM((GROUP, rows, 128), jnp.float32),
            pltpu.VMEM((GROUP, rows, 128), jnp.float32),
            pltpu.VMEM((GROUP, rows, HD), jnp.float32),
            pltpu.VMEM((rows, GROUP * HD), jnp.bfloat16),
            pltpu.VMEM((rows, ROWS), jnp.float32),
            pltpu.SemaphoreType.DMA((8,)),
        ],
        compiler_params=pltpu.CompilerParams(vmem_limit_bytes=36 * MIB),
        cost_estimate=pl.CostEstimate(
            flops=3_000_000_000, bytes_accessed=24 * MIB, transcendentals=3_000_000
        ),
        name=f"attend_{part}",
    )(starts, queries, own, other, keep, weight)
    return outs


def swap(array, flip):
    return lax.ppermute(array, "tp", [(i, i ^ flip) for i in range(8)])


def flows(outs):
    return [(outs[2 * s], outs[2 * s + 1]) for s in range(3)]


def exchange(state, step):
    return [swap(state[s][1], LINK_FLIPS[SET_LINKS[s][step]]) for s in range(3)]


def fold(state, got):
    result = []
    for (keep, _), other in zip(state, got):
        held = (keep.astype(jnp.float32) + other.astype(jnp.float32)).astype(jnp.bfloat16)
        half = held.shape[0] // 2
        result.append((held[:half], held[half:]) if half else held[0])
    return result


def after(first, second):
    return lax.optimization_barrier((first, second))


def body(queries, key_proj, value_proj, out_weight, doc_ids, drop_seed):
    own = pack(key_proj, value_proj)
    column = [own]
    for chips in range(1, 5):
        pairs = [(i, (i + 2 * chips) % 16) for i in range(16)]
        column.append(lax.ppermute(own, "ctx", pairs))
    column = jnp.stack(column)
    keep, starts = keep_masks(drop_seed, doc_ids.reshape(32, 128))
    column, keep = after(column, keep)
    other = lax.ppermute(column, "ctx", [(i, i ^ 1) for i in range(16)])

    rows = ROWS // 2
    state0 = flows(attend(0, rows, starts, queries, column, other, keep, out_weight))
    got0 = exchange(state0, 0)
    keep, state0 = after(keep, state0)
    state1 = flows(attend(1, rows, starts, queries, column, other, keep, out_weight))
    state1, got0 = after(state1, got0)
    state0 = fold(state0, got0)
    got0 = exchange(state0, 1)
    got1 = exchange(state1, 0)
    state0 = fold(state0, got0)
    state1 = fold(state1, got1)
    state1, state0 = after(state1, state0)
    got0 = exchange(state0, 2)
    got1 = exchange(state1, 1)
    state0 = fold(state0, got0)
    state1 = fold(state1, got1)
    got1 = exchange(state1, 2)
    state1 = fold(state1, got1)
    return jnp.concatenate(
        [jnp.concatenate(state0, axis=1), jnp.concatenate(state1, axis=1)], axis=0
    )


def solution(mesh):
    in_specs = (P("ctx", "tp"), P("ctx", "tp"), P("ctx", "tp"), P("tp", None), P(), P())
    return jax.shard_map(
        body, mesh=mesh, in_specs=in_specs, out_specs=P("ctx", "tp"), check_vma=False
    )
```

```python
import functools
import math

import jax
import jax.numpy as jnp
from jax import lax
from jax.experimental import pallas as pl
from jax.experimental.pallas import tpu as pltpu
from jax.sharding import PartitionSpec as P

HEADS = 64
KVH = 8
HD = 128
GROUP = HEADS // KVH
ROWS = 256
BACK = 8
STEP = 3
STEPS = (BACK + STEP) // STEP
PART = ROWS // 2
QUERY_SCALE = HD ** (-0.5) * math.log2(math.e)
INT_MIN = -(1 << 31)
KEEP_FLIP = 0x1999 + INT_MIN
KEEP_BOUND = (1677722 << 8) + INT_MIN
COLUMNS = 1024
SET_COLUMNS = (((0, 384), (384, 768), (768, 1024)), ((0, 384), (384, 640), (640, 1024)))
LINK_FLIPS = (1, 3, 4)
SET_LINKS = ((0, 1, 2), (1, 2, 0), (2, 0, 1))
MIB = 1 << 20


def xor_shift(value):
    return value ^ lax.shift_right_logical(value, jnp.int32(16))


def mixing(value):
    value = xor_shift(value) * 73244475
    value = xor_shift(value) * 73244475
    return xor_shift(value)


def pack(k, v):
    side = lax.broadcasted_iota(jnp.int32, (2, ROWS, HD), 0)
    return jnp.where(side == 0, k[None], v[None])


def in_hbm(array):
    return pltpu.with_memory_space_constraint(array, pltpu.HBM)


def row_low(starts, row):
    low = jnp.zeros_like(row)
    for v in range(1, 8):
        low = jnp.maximum(low, jnp.where(row >= starts[v], starts[v], 0))
    return low


def slot_flip(slot):
    return (slot & 1) ^ (3 * ((slot >> 1) & 1)) ^ (4 * (slot >> 2))


def prepare_body(seed_ref, docs_hbm, q_hbm, w_hbm, keep, query, weight, starts, docs, q, row_hash, sems):
    ctx = lax.axis_index("ctx")
    tp = lax.axis_index("tp")
    docs_copy = pltpu.make_async_copy(docs_hbm, docs, sems.at[8])
    docs_copy.start()
    q_copy = pltpu.make_async_copy(q_hbm, q, sems.at[9])
    q_copy.start()
    w_copies = []
    for slot in range(8):
        column = pl.multiple_of((tp ^ slot_flip(slot)) * COLUMNS, COLUMNS)
        w_copies.append(
            pltpu.make_async_copy(
                w_hbm.at[:, pl.ds(column, COLUMNS)], weight.at[slot], sems.at[slot]
            )
        )
        w_copies[-1].start()

    row0 = ctx * ROWS
    head0 = tp * GROUP
    seed = seed_ref[0]
    rows = row0 + lax.broadcasted_iota(jnp.int32, (ROWS, 128), 0)
    lanes = lax.broadcasted_iota(jnp.int32, (ROWS, 128), 1)
    for h in range(GROUP):
        head_hash = mixing(jnp.full((8, 128), seed * 7919 + head0 + h, jnp.int32))[:1]
        row_hash[h] = mixing(head_hash ^ (rows * 65537)) + lanes
    docs_copy.wait()
    starts[0] = 0
    for v in range(1, 8):
        starts[v] = jnp.sum((docs[...] < v).astype(jnp.int32))
    n = (row0 - (row_low(starts, row0) & -ROWS)) // ROWS

    def step(t, _):
        for u in range(STEP):
            start = row0 - (STEP * t + u) * ROWS
            used = STEP * t + u <= n

            @pl.when(used)
            def _():
                def head(h, _):
                    for part in range(2):
                        for half in range(2):
                            value = row_hash[h, part * PART : (part + 1) * PART] + (start + half * 128)
                            value = xor_shift(value) * 73244475
                            value = xor_shift(value) * 73244475
                            kept = (value ^ KEEP_FLIP) >= KEEP_BOUND
                            lane = u * ROWS + half * 128
                            keep[t, part, pl.ds(h * PART, PART), lane : lane + 128] = jnp.where(
                                kept, jnp.float32(1), jnp.float32(0)
                            ).astype(jnp.bfloat16)
                    return 0

                lax.fori_loop(0, GROUP, head, 0)

            @pl.when(jnp.logical_not(used))
            def _():
                keep[t, :, :, u * ROWS : (u + 1) * ROWS] = jnp.zeros((2, GROUP * PART, ROWS), jnp.bfloat16)

        return 0

    lax.fori_loop(0, n // STEP + 1, step, 0)
    q_copy.wait()
    for part in range(2):
        for h in range(GROUP):
            scaled = q[part * PART : (part + 1) * PART, h * HD : (h + 1) * HD].astype(jnp.float32)
            scaled = scaled * QUERY_SCALE
            high = scaled.astype(jnp.bfloat16)
            query[part, h * PART : (h + 1) * PART, :HD] = high
            query[part, h * PART : (h + 1) * PART, HD:] = (scaled - high.astype(jnp.float32)).astype(
                jnp.bfloat16
            )
    for copy in w_copies:
        copy.wait()


def prepare(seed, docs, queries, weight):
    vmem = pl.BlockSpec(memory_space=pltpu.VMEM)
    hbm = pl.BlockSpec(memory_space=pltpu.HBM)
    smem = pl.BlockSpec(memory_space=pltpu.SMEM)
    return pl.pallas_call(
        prepare_body,
        out_shape=[
            jax.ShapeDtypeStruct((STEPS, 2, GROUP * PART, STEP * ROWS), jnp.bfloat16),
            jax.ShapeDtypeStruct((2, GROUP * PART, 2 * HD), jnp.bfloat16),
            jax.ShapeDtypeStruct((8, GROUP * HD, COLUMNS), jnp.bfloat16),
            jax.ShapeDtypeStruct((8,), jnp.int32),
        ],
        in_specs=[smem, hbm, hbm, hbm],
        out_specs=[vmem, vmem, vmem, smem],
        scratch_shapes=[
            pltpu.VMEM((32, 128), jnp.int32),
            pltpu.VMEM((ROWS, GROUP * HD), jnp.bfloat16),
            pltpu.VMEM((GROUP, ROWS, 128), jnp.int32),
            pltpu.SemaphoreType.DMA((10,)),
        ],
        compiler_params=pltpu.CompilerParams(vmem_limit_bytes=4 * MIB),
        cost_estimate=pl.CostEstimate(
            flops=400_000_000, bytes_accessed=28 * MIB, transcendentals=0
        ),
        name="prepare",
    )(seed, docs, queries, weight)


def attend_body(part, starts, query, own, other, keep, weight, *refs):
    outs = refs[:6]
    keys, values, score, peak, total, accum, mixed, bias = refs[6:]
    ctx = lax.axis_index("ctx")
    block0 = ctx * ROWS
    row0 = block0 + part * PART
    core = ctx & 1
    n = (block0 - (row_low(starts, block0) & -ROWS)) // ROWS
    last_low = row_low(starts, row0 + PART - 1)

    peak[...] = jnp.full(peak.shape, -3e38, jnp.float32)
    total[...] = jnp.zeros(total.shape, jnp.float32)
    accum[...] = jnp.zeros(accum.shape, jnp.float32)
    for d in range(BACK + 1):
        t, lane = d // STEP, d % STEP * ROWS
        source, at = (other, (d + 1) // 2 - core) if d % 2 else (own, d // 2)
        turned = source[at, 0].T
        keys[t, :HD, lane : lane + ROWS] = turned
        keys[t, HD:, lane : lane + ROWS] = turned
        values[t, lane : lane + ROWS] = source[at, 1]

    def score_step(t, masked):
        value = jnp.dot(query[part], keys[t], preferred_element_type=jnp.float32)
        if masked:
            lane = lax.broadcasted_iota(jnp.int32, (PART, STEP * ROWS), 1)
            key_pos = block0 - STEP * t * ROWS - (lane & -ROWS) + (lane & (ROWS - 1))
            row_pos = row0 + lax.broadcasted_iota(jnp.int32, (PART, 1), 0)
            allowed = (key_pos >= row_low(starts, row_pos)) & (key_pos <= row_pos)
            bias[...] = jnp.where(allowed, jnp.float32(0), jnp.float32(-1e30))
            value = value.reshape(GROUP, PART, STEP * ROWS) + bias[...][None]
            value = value.reshape(GROUP * PART, STEP * ROWS)
        score[t] = value
        top = peak[...]
        for k in range(STEP * ROWS // 128):
            top = jnp.maximum(top, value[:, k * 128 : (k + 1) * 128])
        peak[...] = top

    def score_loop(t, _):
        free = (t > 0) & (block0 - (STEP * t + STEP - 1) * ROWS >= last_low)

        @pl.when(free)
        def _():
            score_step(t, False)

        @pl.when(jnp.logical_not(free))
        def _():
            score_step(t, True)

        return 0

    lax.fori_loop(0, n // STEP + 1, score_loop, 0)
    peak[...] = jnp.broadcast_to(jnp.max(peak[...], axis=1, keepdims=True), peak.shape)

    def value_loop(t, _):
        top = peak[...]
        added = total[...]
        probs = []
        for k in range(STEP * ROWS // 128):
            prob = jnp.exp2(score[t, :, k * 128 : (k + 1) * 128] - top)
            added = added + prob
            probs.append(prob.astype(jnp.bfloat16))
        total[...] = added
        prob = jnp.concatenate(probs, axis=1) * keep[t, part]
        accum[...] = accum[...] + jnp.dot(prob, values[t], preferred_element_type=jnp.float32)
        return 0

    lax.fori_loop(0, n // STEP + 1, value_loop, 0)
    for h in range(GROUP):
        at = slice(h * PART, (h + 1) * PART)
        row_sum = jnp.sum(total[at], axis=1, keepdims=True) * 0.9
        mixed[:, h * HD : (h + 1) * HD] = (accum[at] / row_sum).astype(jnp.bfloat16)

    for slot in range(8):
        product = jnp.dot(mixed[...], weight[slot], preferred_element_type=jnp.float32)
        product = product.astype(jnp.bfloat16)
        bits = [(slot >> k) & 1 for k in range(3)]
        for s, (lo, hi) in enumerate(SET_COLUMNS[part]):
            one, two, three = (bits[k] for k in SET_LINKS[s])
            outs[2 * s + one][2 * two + three] = product[:, lo:hi]


def attend(part, starts, query, own, other, keep, weight):
    vmem = pl.BlockSpec(memory_space=pltpu.VMEM)
    out_shape = []
    for lo, hi in SET_COLUMNS[part]:
        out_shape += [jax.ShapeDtypeStruct((4, PART, hi - lo), jnp.bfloat16)] * 2
    heads_rows = GROUP * PART
    return pl.pallas_call(
        functools.partial(attend_body, part),
        out_shape=out_shape,
        in_specs=[pl.BlockSpec(memory_space=pltpu.SMEM)] + [vmem] * 5,
        out_specs=[vmem] * 6,
        scratch_shapes=[
            pltpu.VMEM((STEPS, 2 * HD, STEP * ROWS), jnp.bfloat16),
            pltpu.VMEM((STEPS, STEP * ROWS, HD), jnp.bfloat16),
            pltpu.VMEM((STEPS, heads_rows, STEP * ROWS), jnp.float32),
            pltpu.VMEM((heads_rows, 128), jnp.float32),
            pltpu.VMEM((heads_rows, 128), jnp.float32),
            pltpu.VMEM((heads_rows, HD), jnp.float32),
            pltpu.VMEM((PART, GROUP * HD), jnp.bfloat16),
            pltpu.VMEM((PART, STEP * ROWS), jnp.float32),
        ],
        compiler_params=pltpu.CompilerParams(vmem_limit_bytes=18 * MIB),
        cost_estimate=pl.CostEstimate(
            flops=3_000_000_000, bytes_accessed=24 * MIB, transcendentals=3_000_000
        ),
        name=f"attend_{part}",
    )(starts, query, own, other, keep, weight)


def swap(array, flip):
    return lax.ppermute(array, "tp", [(i, i ^ flip) for i in range(8)])


def flows(outs):
    return [(outs[2 * s], outs[2 * s + 1]) for s in range(3)]


def exchange(state, step):
    return [swap(state[s][1], LINK_FLIPS[SET_LINKS[s][step]]) for s in range(3)]


def fold(state, got):
    result = []
    for (keep, _), other in zip(state, got):
        held = (keep.astype(jnp.float32) + other.astype(jnp.float32)).astype(jnp.bfloat16)
        half = held.shape[0] // 2
        result.append((held[:half], held[half:]) if half else held[0])
    return result


def after(first, second):
    return lax.optimization_barrier((first, second))


def body(queries, key_proj, value_proj, out_weight, doc_ids, drop_seed):
    own = pack(key_proj, value_proj)
    column = [own]
    for chips in range(1, 5):
        pairs = [(i, (i + 2 * chips) % 16) for i in range(16)]
        column.append(lax.ppermute(own, "ctx", pairs))
    column = jnp.stack(column)
    keep, query, weight, starts = prepare(
        drop_seed, in_hbm(doc_ids.reshape(32, 128)), in_hbm(queries), in_hbm(out_weight)
    )
    column, keep = after(column, keep)
    other = lax.ppermute(column, "ctx", [(i, i ^ 1) for i in range(16)])

    state0 = flows(attend(0, starts, query, column, other, keep, weight))
    got0 = exchange(state0, 0)
    keep, state0 = after(keep, state0)
    state1 = flows(attend(1, starts, query, column, other, keep, weight))
    state1, got0 = after(state1, got0)
    state0 = fold(state0, got0)
    got0 = exchange(state0, 1)
    got1 = exchange(state1, 0)
    state0 = fold(state0, got0)
    state1 = fold(state1, got1)
    state1, state0 = after(state1, state0)
    got0 = exchange(state0, 2)
    got1 = exchange(state1, 1)
    state0 = fold(state0, got0)
    state1 = fold(state1, got1)
    got1 = exchange(state1, 2)
    state1 = fold(state1, got1)
    return jnp.concatenate(
        [jnp.concatenate(state0, axis=1), jnp.concatenate(state1, axis=1)], axis=0
    )


def solution(mesh):
    in_specs = (P("ctx", "tp"), P("ctx", "tp"), P("ctx", "tp"), P("tp", None), P(), P())
    return jax.shard_map(
        body, mesh=mesh, in_specs=in_specs, out_specs=P("ctx", "tp"), check_vma=False
    )
```

```python
import functools
import math

import jax
import jax.numpy as jnp
from jax import lax
from jax.experimental import pallas as pl
from jax.experimental.pallas import tpu as pltpu
from jax.sharding import PartitionSpec as P

HEADS = 64
KVH = 8
HD = 128
GROUP = HEADS // KVH
ROWS = 256
BACK = 8
STEP = 3
STEPS = (BACK + STEP) // STEP
PART = ROWS // 2
QUERY_SCALE = HD ** (-0.5) * math.log2(math.e)
INT_MIN = -(1 << 31)
KEEP_FLIP = 0x1999 + INT_MIN
KEEP_BOUND = (1677722 << 8) + INT_MIN
COLUMNS = 1024
LINK_FLIPS = (1, 3, 4)
THIRDS = ((0, 96, (0, 3, 6, 8)), (96, 80, (0, 3, 5, 8)), (176, 80, (0, 2, 5, 8)))
SET_LINKS = ((0, 1, 2), (1, 2, 0), (2, 0, 1))
MIB = 1 << 20
LANES = 128


def units(s):
    found, offset = [], 0
    for row, count, cuts in THIRDS:
        for unit in range(cuts[s], cuts[s + 1]):
            found.append((row, count, unit, offset))
            offset += count
    return found, offset


def xor_shift(value):
    return value ^ lax.shift_right_logical(value, jnp.int32(16))


def mixing(value):
    value = xor_shift(value) * 73244475
    value = xor_shift(value) * 73244475
    return xor_shift(value)


def pack(k, v):
    side = lax.broadcasted_iota(jnp.int32, (2, ROWS, HD), 0)
    return jnp.where(side == 0, k[None], v[None])


def in_hbm(array):
    return pltpu.with_memory_space_constraint(array, pltpu.HBM)


def row_low(starts, row):
    low = jnp.zeros_like(row)
    for v in range(1, 8):
        low = jnp.maximum(low, jnp.where(row >= starts[v], starts[v], 0))
    return low


def slot_flip(slot):
    return (slot & 1) ^ (3 * ((slot >> 1) & 1)) ^ (4 * (slot >> 2))


def prepare_body(seed_ref, docs_hbm, q_hbm, w_hbm, keep, query, weight, starts, docs, q, row_hash, sems):
    ctx = lax.axis_index("ctx")
    tp = lax.axis_index("tp")
    docs_copy = pltpu.make_async_copy(docs_hbm, docs, sems.at[8])
    docs_copy.start()
    q_copy = pltpu.make_async_copy(q_hbm, q, sems.at[9])
    q_copy.start()
    w_copies = []
    for slot in range(8):
        column = pl.multiple_of((tp ^ slot_flip(slot)) * COLUMNS, COLUMNS)
        w_copies.append(
            pltpu.make_async_copy(
                w_hbm.at[:, pl.ds(column, COLUMNS)], weight.at[slot], sems.at[slot]
            )
        )
        w_copies[-1].start()

    row0 = ctx * ROWS
    head0 = tp * GROUP
    seed = seed_ref[0]
    rows = row0 + lax.broadcasted_iota(jnp.int32, (ROWS, 128), 0)
    lanes = lax.broadcasted_iota(jnp.int32, (ROWS, 128), 1)
    for h in range(GROUP):
        head_hash = mixing(jnp.full((8, 128), seed * 7919 + head0 + h, jnp.int32))[:1]
        row_hash[h] = mixing(head_hash ^ (rows * 65537)) + lanes
    docs_copy.wait()
    starts[0] = 0
    for v in range(1, 8):
        starts[v] = jnp.sum((docs[...] < v).astype(jnp.int32))
    n = (row0 - (row_low(starts, row0) & -ROWS)) // ROWS

    def step(t, _):
        for u in range(STEP):
            start = row0 - (STEP * t + u) * ROWS
            used = STEP * t + u <= n

            @pl.when(used)
            def _():
                def head(h, _):
                    for part in range(2):
                        for half in range(2):
                            value = row_hash[h, part * PART : (part + 1) * PART] + (start + half * 128)
                            value = xor_shift(value) * 73244475
                            value = xor_shift(value) * 73244475
                            kept = (value ^ KEEP_FLIP) >= KEEP_BOUND
                            lane = u * ROWS + half * 128
                            keep[t, part, pl.ds(h * PART, PART), lane : lane + 128] = jnp.where(
                                kept, jnp.float32(1), jnp.float32(0)
                            ).astype(jnp.bfloat16)
                    return 0

                lax.fori_loop(0, GROUP, head, 0)

            @pl.when(jnp.logical_not(used))
            def _():
                keep[t, :, :, u * ROWS : (u + 1) * ROWS] = jnp.zeros((2, GROUP * PART, ROWS), jnp.bfloat16)

        return 0

    lax.fori_loop(0, n // STEP + 1, step, 0)
    q_copy.wait()
    for part in range(2):
        for h in range(GROUP):
            scaled = q[part * PART : (part + 1) * PART, h * HD : (h + 1) * HD].astype(jnp.float32)
            scaled = scaled * QUERY_SCALE
            high = scaled.astype(jnp.bfloat16)
            query[part, h * PART : (h + 1) * PART, :HD] = high
            query[part, h * PART : (h + 1) * PART, HD:] = (scaled - high.astype(jnp.float32)).astype(
                jnp.bfloat16
            )
    for copy in w_copies:
        copy.wait()


def prepare(seed, docs, queries, weight):
    vmem = pl.BlockSpec(memory_space=pltpu.VMEM)
    hbm = pl.BlockSpec(memory_space=pltpu.HBM)
    smem = pl.BlockSpec(memory_space=pltpu.SMEM)
    return pl.pallas_call(
        prepare_body,
        out_shape=[
            jax.ShapeDtypeStruct((STEPS, 2, GROUP * PART, STEP * ROWS), jnp.bfloat16),
            jax.ShapeDtypeStruct((2, GROUP * PART, 2 * HD), jnp.bfloat16),
            jax.ShapeDtypeStruct((8, GROUP * HD, COLUMNS), jnp.bfloat16),
            jax.ShapeDtypeStruct((8,), jnp.int32),
        ],
        in_specs=[smem, hbm, hbm, hbm],
        out_specs=[vmem, vmem, vmem, smem],
        scratch_shapes=[
            pltpu.VMEM((32, 128), jnp.int32),
            pltpu.VMEM((ROWS, GROUP * HD), jnp.bfloat16),
            pltpu.VMEM((GROUP, ROWS, 128), jnp.int32),
            pltpu.SemaphoreType.DMA((10,)),
        ],
        compiler_params=pltpu.CompilerParams(vmem_limit_bytes=4 * MIB),
        cost_estimate=pl.CostEstimate(
            flops=400_000_000, bytes_accessed=28 * MIB, transcendentals=0
        ),
        name="prepare",
    )(seed, docs, queries, weight)


def project_body(targets, mixed, weight, outs):
    for (s, side), out in zip(targets, outs):
        found, _ = units(s)
        low = min(unit for _, _, unit, _ in found)
        high = max(unit for _, _, unit, _ in found) + 1
        for slot in range(8):
            one, two, three = ((slot >> k) & 1 for k in SET_LINKS[s])
            if one != side:
                continue
            product = jnp.dot(
                mixed[...], weight[slot, :, low * LANES : high * LANES], preferred_element_type=jnp.float32
            ).astype(jnp.bfloat16)
            for row, count, unit, offset in found:
                lane = (unit - low) * LANES
                out[2 * two + three, offset : offset + count] = product[
                    row : row + count, lane : lane + LANES
                ]


def project_shapes(targets):
    return [jax.ShapeDtypeStruct((4, units(s)[1], LANES), jnp.bfloat16) for s, _ in targets]


def project(name, targets, mixed, weight):
    vmem = pl.BlockSpec(memory_space=pltpu.VMEM)

    def kernel(mixed, weight, *outs):
        project_body(targets, mixed, weight, outs)

    return pl.pallas_call(
        kernel,
        out_shape=project_shapes(targets),
        in_specs=[vmem] * 2,
        out_specs=[vmem] * len(targets),
        compiler_params=pltpu.CompilerParams(vmem_limit_bytes=4 * MIB),
        cost_estimate=pl.CostEstimate(
            flops=700_000_000 * len(targets), bytes_accessed=4 * MIB, transcendentals=0
        ),
        name=name,
    )(mixed, weight)


def attend_body(targets, starts, query, own, other, keep, weight, mixed, *refs):
    sends = refs[: len(targets)]
    keys, values, score, peak, total, accum, bias = refs[len(targets) :]
    ctx = lax.axis_index("ctx")
    block0 = ctx * ROWS
    core = ctx & 1
    n = (block0 - (row_low(starts, block0) & -ROWS)) // ROWS

    for d in range(BACK + 1):
        t, lane = d // STEP, d % STEP * ROWS
        source, at = (other, (d + 1) // 2 - core) if d % 2 else (own, d // 2)
        turned = source[at, 0].T
        keys[t, :HD, lane : lane + ROWS] = turned
        keys[t, HD:, lane : lane + ROWS] = turned
        values[t, lane : lane + ROWS] = source[at, 1]

    for part in range(2):
        row0 = block0 + part * PART
        last_low = row_low(starts, row0 + PART - 1)
        peak[...] = jnp.full(peak.shape, -3e38, jnp.float32)
        total[...] = jnp.zeros(total.shape, jnp.float32)
        accum[...] = jnp.zeros(accum.shape, jnp.float32)

        def score_step(t, masked):
            value = jnp.dot(query[part], keys[t], preferred_element_type=jnp.float32)
            if masked:
                lane = lax.broadcasted_iota(jnp.int32, (PART, STEP * ROWS), 1)
                key_pos = block0 - STEP * t * ROWS - (lane & -ROWS) + (lane & (ROWS - 1))
                row_pos = row0 + lax.broadcasted_iota(jnp.int32, (PART, 1), 0)
                allowed = (key_pos >= row_low(starts, row_pos)) & (key_pos <= row_pos)
                bias[...] = jnp.where(allowed, jnp.float32(0), jnp.float32(-1e30))
                value = value.reshape(GROUP, PART, STEP * ROWS) + bias[...][None]
                value = value.reshape(GROUP * PART, STEP * ROWS)
            score[t] = value
            top = peak[...]
            for k in range(STEP * ROWS // 128):
                top = jnp.maximum(top, value[:, k * 128 : (k + 1) * 128])
            peak[...] = top

        def score_loop(t, _):
            free = (t > 0) & (block0 - (STEP * t + STEP - 1) * ROWS >= last_low)

            @pl.when(free)
            def _():
                score_step(t, False)

            @pl.when(jnp.logical_not(free))
            def _():
                score_step(t, True)

            return 0

        lax.fori_loop(0, n // STEP + 1, score_loop, 0)
        peak[...] = jnp.broadcast_to(jnp.max(peak[...], axis=1, keepdims=True), peak.shape)

        def value_loop(t, _):
            top = peak[...]
            added = total[...]
            probs = []
            for k in range(STEP * ROWS // 128):
                prob = jnp.exp2(score[t, :, k * 128 : (k + 1) * 128] - top)
                added = added + prob
                probs.append(prob.astype(jnp.bfloat16))
            total[...] = added
            prob = jnp.concatenate(probs, axis=1) * keep[t, part]
            accum[...] = accum[...] + jnp.dot(prob, values[t], preferred_element_type=jnp.float32)
            return 0

        lax.fori_loop(0, n // STEP + 1, value_loop, 0)
        for h in range(GROUP):
            at = slice(h * PART, (h + 1) * PART)
            row_sum = jnp.sum(total[at], axis=1, keepdims=True) * 0.9
            mixed[part * PART : (part + 1) * PART, h * HD : (h + 1) * HD] = (
                accum[at] / row_sum
            ).astype(jnp.bfloat16)

    project_body(targets, mixed, weight, sends)


def attend(targets, starts, query, own, other, keep, weight):
    vmem = pl.BlockSpec(memory_space=pltpu.VMEM)
    heads_rows = GROUP * PART
    return pl.pallas_call(
        functools.partial(attend_body, targets),
        out_shape=[jax.ShapeDtypeStruct((ROWS, GROUP * HD), jnp.bfloat16)] + project_shapes(targets),
        in_specs=[pl.BlockSpec(memory_space=pltpu.SMEM)] + [vmem] * 5,
        out_specs=[vmem] * (1 + len(targets)),
        scratch_shapes=[
            pltpu.VMEM((STEPS, 2 * HD, STEP * ROWS), jnp.bfloat16),
            pltpu.VMEM((STEPS, STEP * ROWS, HD), jnp.bfloat16),
            pltpu.VMEM((STEPS, heads_rows, STEP * ROWS), jnp.float32),
            pltpu.VMEM((heads_rows, 128), jnp.float32),
            pltpu.VMEM((heads_rows, 128), jnp.float32),
            pltpu.VMEM((heads_rows, HD), jnp.float32),
            pltpu.VMEM((PART, STEP * ROWS), jnp.float32),
        ],
        compiler_params=pltpu.CompilerParams(vmem_limit_bytes=18 * MIB),
        cost_estimate=pl.CostEstimate(
            flops=4_000_000_000, bytes_accessed=24 * MIB, transcendentals=6_000_000
        ),
        name="attend",
    )(starts, query, own, other, keep, weight)


def finish_body(*refs):
    out = refs[6]
    for s in range(3):
        for row, count, unit, offset in units(s)[0]:
            held = refs[2 * s][0, offset : offset + count].astype(jnp.float32)
            held = held + refs[2 * s + 1][0, offset : offset + count].astype(jnp.float32)
            out[row : row + count, unit * LANES : (unit + 1) * LANES] = held.astype(jnp.bfloat16)


def finish(pairs):
    vmem = pl.BlockSpec(memory_space=pltpu.VMEM)
    return pl.pallas_call(
        finish_body,
        out_shape=jax.ShapeDtypeStruct((ROWS, COLUMNS), jnp.bfloat16),
        in_specs=[vmem] * 6,
        out_specs=vmem,
        compiler_params=pltpu.CompilerParams(vmem_limit_bytes=4 * MIB),
        name="finish",
    )(*pairs)


def swap(array, flip):
    return lax.ppermute(array, "tp", [(i, i ^ flip) for i in range(8)])


def after(first, second):
    return lax.optimization_barrier((first, second))


def body(queries, key_proj, value_proj, out_weight, doc_ids, drop_seed):
    own = lax.optimization_barrier(pack(key_proj, value_proj))
    column = [own]
    for chips in range(1, 5):
        pairs = [(i, (i + 2 * chips) % 16) for i in range(16)]
        column.append(lax.ppermute(own, "ctx", pairs))
    column = jnp.stack(column)
    keep, query, weight, starts = prepare(
        drop_seed, in_hbm(doc_ids.reshape(32, 128)), in_hbm(queries), in_hbm(out_weight)
    )
    column, keep = after(column, keep)
    other = lax.ppermute(column, "ctx", [(i, i ^ 1) for i in range(16)])

    sent, rest, got = [None] * 3, [None] * 3, [None] * 3
    mixed, sent[0] = attend(((0, 1),), starts, query, column, other, keep, weight)
    got[0] = swap(sent[0], LINK_FLIPS[SET_LINKS[0][0]])
    for s in (1, 2):
        mixed, sent[s - 1] = after(mixed, sent[s - 1])
        (sent[s],) = project(f"send_{s}", ((s, 1),), mixed, weight)
        got[s] = swap(sent[s], LINK_FLIPS[SET_LINKS[s][0]])
    mixed, sent[2] = after(mixed, sent[2])
    rest = list(project("rest", ((0, 0), (1, 0), (2, 0)), mixed, weight))
    order = mixed
    for step in (1, 2):
        for s in range(3):
            rest[s], got[s], order = lax.optimization_barrier((rest[s], got[s], order))
            held = (rest[s].astype(jnp.float32) + got[s].astype(jnp.float32)).astype(jnp.bfloat16)
            half = held.shape[0] // 2
            rest[s], order = held[:half], held[half:]
            got[s] = swap(order, LINK_FLIPS[SET_LINKS[s][step]])
    return finish([array for s in range(3) for array in (rest[s], got[s])])


def solution(mesh):
    in_specs = (P("ctx", "tp"), P("ctx", "tp"), P("ctx", "tp"), P("tp", None), P(), P())
    return jax.shard_map(
        body, mesh=mesh, in_specs=in_specs, out_specs=P("ctx", "tp"), check_vma=False
    )
```

```python
import functools
import math

import jax
import jax.numpy as jnp
from jax import lax
from jax.experimental import pallas as pl
from jax.experimental.pallas import tpu as pltpu
from jax.sharding import PartitionSpec as P

HEADS = 64
KVH = 8
HD = 128
GROUP = HEADS // KVH
ROWS = 256
BACK = 8
STEP = 3
STEPS = (BACK + STEP) // STEP
QUERY_SCALE = HD ** (-0.5) * math.log2(math.e)
INT_MIN = -(1 << 31)
KEEP_FLIP = 0x1999 + INT_MIN
KEEP_BOUND = (1677722 << 8) + INT_MIN
COLUMNS = 1024
LINK_FLIPS = (1, 3, 4)
SIZES = (144, 112)
BEGINS = (0, 144)
THIRDS = (
    ((0, 48, (0, 3, 6, 8)), (48, 48, (0, 3, 5, 8)), (96, 48, (0, 2, 5, 8))),
    ((0, 48, (0, 3, 6, 8)), (48, 32, (0, 3, 5, 8)), (80, 32, (0, 2, 5, 8))),
)
SET_LINKS = ((0, 1, 2), (1, 2, 0), (2, 0, 1))
MIB = 1 << 20
LANES = 128


def units(s, parts):
    found, offset = [], 0
    for part in parts:
        for row, count, cuts in THIRDS[part]:
            for unit in range(cuts[s], cuts[s + 1]):
                found.append((BEGINS[part] + row, count, unit, offset))
                offset += count
    return found, offset


def xor_shift(value):
    return value ^ lax.shift_right_logical(value, jnp.int32(16))


def mixing(value):
    value = xor_shift(value) * 73244475
    value = xor_shift(value) * 73244475
    return xor_shift(value)


def pack_body(k_hbm, v_hbm, out, k, sems):
    k_copy = pltpu.make_async_copy(k_hbm, k, sems.at[0])
    v_copy = pltpu.make_async_copy(v_hbm, out.at[1], sems.at[1])
    k_copy.start()
    v_copy.start()
    k_copy.wait()
    turned = k[...].T
    out[0, :HD] = turned[:, :128]
    out[0, HD:] = turned[:, 128:]
    v_copy.wait()


def pack(k, v):
    return pl.pallas_call(
        pack_body,
        out_shape=jax.ShapeDtypeStruct((2, ROWS, HD), jnp.bfloat16),
        in_specs=[pl.BlockSpec(memory_space=pltpu.HBM)] * 2,
        out_specs=pl.BlockSpec(memory_space=pltpu.VMEM),
        scratch_shapes=[pltpu.VMEM((ROWS, HD), jnp.bfloat16), pltpu.SemaphoreType.DMA((2,))],
        compiler_params=pltpu.CompilerParams(vmem_limit_bytes=1 * MIB),
        name="pack",
    )(in_hbm(k), in_hbm(v))


def in_hbm(array):
    return pltpu.with_memory_space_constraint(array, pltpu.HBM)


def row_low(starts, row):
    low = jnp.zeros_like(row)
    for v in range(1, 8):
        low = jnp.maximum(low, jnp.where(row >= starts[v], starts[v], 0))
    return low


def slot_flip(slot):
    return (slot & 1) ^ (3 * ((slot >> 1) & 1)) ^ (4 * (slot >> 2))


def prepare_body(seed_ref, docs_hbm, q_hbm, w_hbm, keep, query, weight, starts, docs, q, row_hash, sems):
    ctx = lax.axis_index("ctx")
    tp = lax.axis_index("tp")
    docs_copy = pltpu.make_async_copy(docs_hbm, docs, sems.at[8])
    docs_copy.start()
    q_copy = pltpu.make_async_copy(q_hbm, q, sems.at[9])
    q_copy.start()
    w_copies = []
    for slot in range(8):
        column = pl.multiple_of((tp ^ slot_flip(slot)) * COLUMNS, COLUMNS)
        w_copies.append(
            pltpu.make_async_copy(
                w_hbm.at[:, pl.ds(column, COLUMNS)], weight.at[slot], sems.at[slot]
            )
        )
        w_copies[-1].start()

    row0 = ctx * ROWS
    head0 = tp * GROUP
    seed = seed_ref[0]
    rows = row0 + lax.broadcasted_iota(jnp.int32, (ROWS, 128), 0)
    lanes = lax.broadcasted_iota(jnp.int32, (ROWS, 128), 1)
    for h in range(GROUP):
        head_hash = mixing(jnp.full((8, 128), seed * 7919 + head0 + h, jnp.int32))[:1]
        row_hash[h] = mixing(head_hash ^ (rows * 65537)) + lanes
    docs_copy.wait()
    starts[0] = 0
    for v in range(1, 8):
        starts[v] = jnp.sum((docs[...] < v).astype(jnp.int32))
    n = (row0 - (row_low(starts, row0) & -ROWS)) // ROWS

    def step(t, _):
        for u in range(STEP):
            start = row0 - (STEP * t + u) * ROWS
            used = STEP * t + u <= n

            @pl.when(used)
            def _():
                def head(h, _):
                    for begin, count in zip(BEGINS, SIZES):
                        for half in range(2):
                            value = row_hash[h, begin : begin + count] + (start + half * 128)
                            value = xor_shift(value) * 73244475
                            value = xor_shift(value) * 73244475
                            kept = (value ^ KEEP_FLIP) >= KEEP_BOUND
                            lane = u * ROWS + half * 128
                            place = pl.ds(GROUP * begin + h * count, count)
                            keep[t, place, lane : lane + 128] = jnp.where(
                                kept, jnp.float32(1), jnp.float32(0)
                            ).astype(jnp.bfloat16)
                    return 0

                lax.fori_loop(0, GROUP, head, 0)

            @pl.when(jnp.logical_not(used))
            def _():
                keep[t, :, u * ROWS : (u + 1) * ROWS] = jnp.zeros((GROUP * ROWS, ROWS), jnp.bfloat16)

        return 0

    lax.fori_loop(0, n // STEP + 1, step, 0)
    q_copy.wait()
    for begin, count in zip(BEGINS, SIZES):
        for h in range(GROUP):
            scaled = q[begin : begin + count, h * HD : (h + 1) * HD].astype(jnp.float32) * QUERY_SCALE
            high = scaled.astype(jnp.bfloat16)
            low = (scaled - high.astype(jnp.float32)).astype(jnp.bfloat16)
            place = slice(GROUP * begin + h * count, GROUP * begin + (h + 1) * count)
            query[place, :HD] = high
            query[place, HD:] = low
    for copy in w_copies:
        copy.wait()


def prepare(seed, docs, queries, weight):
    vmem = pl.BlockSpec(memory_space=pltpu.VMEM)
    hbm = pl.BlockSpec(memory_space=pltpu.HBM)
    smem = pl.BlockSpec(memory_space=pltpu.SMEM)
    return pl.pallas_call(
        prepare_body,
        out_shape=[
            jax.ShapeDtypeStruct((STEPS, GROUP * ROWS, STEP * ROWS), jnp.bfloat16),
            jax.ShapeDtypeStruct((GROUP * ROWS, 2 * HD), jnp.bfloat16),
            jax.ShapeDtypeStruct((8, GROUP * HD, COLUMNS), jnp.bfloat16),
            jax.ShapeDtypeStruct((8,), jnp.int32),
        ],
        in_specs=[smem, hbm, hbm, hbm],
        out_specs=[vmem, vmem, vmem, smem],
        scratch_shapes=[
            pltpu.VMEM((32, 128), jnp.int32),
            pltpu.VMEM((ROWS, GROUP * HD), jnp.bfloat16),
            pltpu.VMEM((GROUP, ROWS, 128), jnp.int32),
            pltpu.SemaphoreType.DMA((10,)),
        ],
        compiler_params=pltpu.CompilerParams(vmem_limit_bytes=4 * MIB),
        cost_estimate=pl.CostEstimate(
            flops=400_000_000, bytes_accessed=28 * MIB, transcendentals=0
        ),
        name="prepare",
    )(seed, docs, queries, weight)


def project_body(side, parts, mixed, weight, outs):
    for s, out in enumerate(outs):
        found, _ = units(s, parts)
        low = min(unit for _, _, unit, _ in found)
        high = max(unit for _, _, unit, _ in found) + 1
        for slot in range(8):
            one, two, three = ((slot >> k) & 1 for k in SET_LINKS[s])
            if one != side:
                continue
            product = jnp.dot(
                mixed, weight[slot, :, low * LANES : high * LANES], preferred_element_type=jnp.float32
            ).astype(jnp.bfloat16)
            for row, count, unit, offset in found:
                row, lane = row - BEGINS[parts[0]], (unit - low) * LANES
                out[2 * two + three, offset : offset + count] = product[
                    row : row + count, lane : lane + LANES
                ]


def slots(count, parts):
    return [jax.ShapeDtypeStruct((count, units(s, parts)[1], LANES), jnp.bfloat16) for s in range(3)]


def rest_body(first, second, weight, *outs):
    mixed = jnp.concatenate([first[...], second[...]], axis=0)
    project_body(0, (0, 1), mixed, weight, outs)


def project_rest(first, second, weight):
    vmem = pl.BlockSpec(memory_space=pltpu.VMEM)
    return pl.pallas_call(
        rest_body,
        out_shape=slots(4, (0, 1)),
        in_specs=[vmem] * 3,
        out_specs=[vmem] * 3,
        compiler_params=pltpu.CompilerParams(vmem_limit_bytes=6 * MIB),
        cost_estimate=pl.CostEstimate(
            flops=2_100_000_000, bytes_accessed=4 * MIB, transcendentals=0
        ),
        name="rest",
    )(first, second, weight)


def turn_body(own, other, keys, values):
    core = lax.axis_index("ctx") & 1
    for d in range(BACK + 1):
        t, lane = d // STEP, d % STEP * ROWS
        source, at = (other, (d + 1) // 2 - core) if d % 2 else (own, d // 2)
        for half in range(2):
            turned = source[at, 0, half * HD : (half + 1) * HD]
            at_lane = slice(lane + half * 128, lane + (half + 1) * 128)
            keys[t, :HD, at_lane] = turned
            keys[t, HD:, at_lane] = turned
        values[t, lane : lane + ROWS] = source[at, 1]


def attend_body(part, starts, query, *refs):
    if part:
        keys, values, keep, weight, mixed, *refs = refs
    else:
        own, other, keep, weight, keys, values, mixed, *refs = refs
        turn_body(own, other, keys, values)
    sends = refs[:3]
    score, peak, total, accum, bias = refs[3:]
    block0 = lax.axis_index("ctx") * ROWS
    n = (block0 - (row_low(starts, block0) & -ROWS)) // ROWS
    rows = SIZES[part]
    row0 = block0 + BEGINS[part]
    span = slice(GROUP * BEGINS[part], GROUP * (BEGINS[part] + rows))
    last_low = row_low(starts, row0 + rows - 1)
    peak[...] = jnp.full(peak.shape, -3e38, jnp.float32)
    total[...] = jnp.zeros(total.shape, jnp.float32)
    accum[...] = jnp.zeros(accum.shape, jnp.float32)

    def score_step(t, masked):
        value = jnp.dot(query[span], keys[t], preferred_element_type=jnp.float32)
        if masked:
            lane = lax.broadcasted_iota(jnp.int32, (rows, STEP * ROWS), 1)
            key_pos = block0 - STEP * t * ROWS - (lane & -ROWS) + (lane & (ROWS - 1))
            row_pos = row0 + lax.broadcasted_iota(jnp.int32, (rows, 1), 0)
            allowed = (key_pos >= row_low(starts, row_pos)) & (key_pos <= row_pos)
            bias[...] = jnp.where(allowed, jnp.float32(0), jnp.float32(-1e30))
            value = value.reshape(GROUP, rows, STEP * ROWS) + bias[...][None]
            value = value.reshape(GROUP * rows, STEP * ROWS)
        score[t] = value
        top = peak[...]
        for k in range(STEP * ROWS // 128):
            top = jnp.maximum(top, value[:, k * 128 : (k + 1) * 128])
        peak[...] = top

    def score_loop(t, _):
        free = (t > 0) & (block0 - (STEP * t + STEP - 1) * ROWS >= last_low)

        @pl.when(free)
        def _():
            score_step(t, False)

        @pl.when(jnp.logical_not(free))
        def _():
            score_step(t, True)

        return 0

    lax.fori_loop(0, n // STEP + 1, score_loop, 0)
    peak[...] = jnp.broadcast_to(jnp.max(peak[...], axis=1, keepdims=True), peak.shape)

    def value_loop(t, _):
        top = peak[...]
        added = total[...]
        probs = []
        for k in range(STEP * ROWS // 128):
            prob = jnp.exp2(score[t, :, k * 128 : (k + 1) * 128] - top)
            added = added + prob
            probs.append(prob.astype(jnp.bfloat16))
        total[...] = added
        prob = jnp.concatenate(probs, axis=1) * keep[t, span]
        accum[...] = accum[...] + jnp.dot(prob, values[t], preferred_element_type=jnp.float32)
        return 0

    lax.fori_loop(0, n // STEP + 1, value_loop, 0)
    for h in range(GROUP):
        at = slice(h * rows, (h + 1) * rows)
        row_sum = jnp.sum(total[at], axis=1, keepdims=True) * 0.9
        mixed[:, h * HD : (h + 1) * HD] = (accum[at] / row_sum).astype(jnp.bfloat16)

    project_body(1, (part,), mixed[...], weight, sends)


def attend(part, starts, query, sources, keep, weight):
    vmem = pl.BlockSpec(memory_space=pltpu.VMEM)
    rows = SIZES[part]
    heads_rows = GROUP * rows
    out_shape = [
        jax.ShapeDtypeStruct((STEPS, 2 * HD, STEP * ROWS), jnp.bfloat16),
        jax.ShapeDtypeStruct((STEPS, STEP * ROWS, HD), jnp.bfloat16),
        jax.ShapeDtypeStruct((rows, GROUP * HD), jnp.bfloat16),
    ] + slots(4, (part,))
    out_shape = out_shape[2 if part else 0 :]
    return pl.pallas_call(
        functools.partial(attend_body, part),
        out_shape=out_shape,
        in_specs=[pl.BlockSpec(memory_space=pltpu.SMEM)] + [vmem] * 5,
        out_specs=[vmem] * len(out_shape),
        scratch_shapes=[
            pltpu.VMEM((STEPS, heads_rows, STEP * ROWS), jnp.float32),
            pltpu.VMEM((heads_rows, 128), jnp.float32),
            pltpu.VMEM((heads_rows, 128), jnp.float32),
            pltpu.VMEM((heads_rows, HD), jnp.float32),
            pltpu.VMEM((rows, STEP * ROWS), jnp.float32),
        ],
        compiler_params=pltpu.CompilerParams(vmem_limit_bytes=16 * MIB),
        cost_estimate=pl.CostEstimate(
            flops=3_000_000_000, bytes_accessed=16 * MIB, transcendentals=3_000_000
        ),
        name=f"attend_{part}",
    )(starts, query, *sources, keep, weight)


def fold_body(count, *refs):
    rest, got, (kept, sent) = refs[0], refs[1:-2], refs[-2:]
    offset = 0
    for other in got:
        rows = other.shape[1]
        for j in range(count):
            held = rest[j, offset : offset + rows].astype(jnp.float32) + other[j].astype(jnp.float32)
            target = kept if j < count // 2 else sent
            target[j % (count // 2), offset : offset + rows] = held.astype(jnp.bfloat16)
        offset += rows


def fold(rest, got):
    vmem = pl.BlockSpec(memory_space=pltpu.VMEM)
    count = rest.shape[0]
    half = jax.ShapeDtypeStruct((count // 2,) + rest.shape[1:], jnp.bfloat16)
    return pl.pallas_call(
        functools.partial(fold_body, count),
        out_shape=[half] * 2,
        in_specs=[vmem] * (1 + len(got)),
        out_specs=[vmem] * 2,
        compiler_params=pltpu.CompilerParams(vmem_limit_bytes=2 * MIB),
        cost_estimate=pl.CostEstimate(flops=300_000, bytes_accessed=MIB, transcendentals=0),
        name=f"fold_{count}",
    )(rest, *got)


def finish_body(*refs):
    out = refs[6]
    for s in range(3):
        for row, count, unit, offset in units(s, (0, 1))[0]:
            held = refs[2 * s][0, offset : offset + count].astype(jnp.float32)
            held = held + refs[2 * s + 1][0, offset : offset + count].astype(jnp.float32)
            out[row : row + count, unit * LANES : (unit + 1) * LANES] = held.astype(jnp.bfloat16)


def finish(pairs):
    vmem = pl.BlockSpec(memory_space=pltpu.VMEM)
    return pl.pallas_call(
        finish_body,
        out_shape=jax.ShapeDtypeStruct((ROWS, COLUMNS), jnp.bfloat16),
        in_specs=[vmem] * 6,
        out_specs=vmem,
        compiler_params=pltpu.CompilerParams(vmem_limit_bytes=4 * MIB),
        name="finish",
    )(*pairs)


def swap(array, flip):
    return lax.ppermute(array, "tp", [(i, i ^ flip) for i in range(8)])


def after(first, second):
    return lax.optimization_barrier((first, second))


def body(queries, key_proj, value_proj, out_weight, doc_ids, drop_seed):
    own = pack(key_proj, value_proj)
    column = [own] * 5
    for chips in (2, 4, 1, 3):
        pairs = [(i, (i + 2 * chips) % 16) for i in range(16)]
        column[chips] = lax.ppermute(own, "ctx", pairs)
    column = jnp.stack(column)
    keep, query, weight, starts = prepare(
        drop_seed, in_hbm(doc_ids.reshape(32, 128)), in_hbm(queries), in_hbm(out_weight)
    )
    column, keep = after(column, keep)
    other = lax.ppermute(column, "ctx", [(i, i ^ 1) for i in range(16)])

    keys, values, first, *sent = attend(0, starts, query, (column, other), keep, weight)
    keep, sent = after(keep, sent)
    got = [[swap(sent[s], LINK_FLIPS[SET_LINKS[s][0]])] for s in range(3)]
    second, *sent = attend(1, starts, query, (keys, values), keep, weight)
    second, sent = after(second, sent)
    for s in range(3):
        sent[s], got[s] = after(sent[s], got[s])
        got[s].append(swap(sent[s], LINK_FLIPS[SET_LINKS[s][0]]))
    rest = list(project_rest(first, second, weight))
    order = second
    for step in (1, 2):
        for s in range(3):
            rest[s], got[s], order = lax.optimization_barrier((rest[s], got[s], order))
            rest[s], order = fold(rest[s], got[s])
            got[s] = [swap(order, LINK_FLIPS[SET_LINKS[s][step]])]
    return finish([array for s in range(3) for array in (rest[s], got[s][0])])


def solution(mesh):
    in_specs = (P("ctx", "tp"), P("ctx", "tp"), P("ctx", "tp"), P("tp", None), P(), P())
    return jax.shard_map(
        body, mesh=mesh, in_specs=in_specs, out_specs=P("ctx", "tp"), check_vma=False
    )
```

```python
import functools
import math

import jax
import jax.numpy as jnp
from jax import lax
from jax.experimental import pallas as pl
from jax.experimental.pallas import tpu as pltpu
from jax.sharding import PartitionSpec as P

HEADS = 64
KVH = 8
HD = 128
GROUP = HEADS // KVH
ROWS = 256
BACK = 8
STEP = 3
STEPS = (BACK + STEP) // STEP
QUERY_SCALE = HD ** (-0.5) * math.log2(math.e)
INT_MIN = -(1 << 31)
KEEP_FLIP = 0x1999 + INT_MIN
KEEP_BOUND = (1677722 << 8) + INT_MIN
COLUMNS = 1024
LINK_FLIPS = (1, 3, 4)
SIZES = (144, 112)
BEGINS = (0, 144)
THIRDS = (
    ((0, 48, (0, 3, 6, 8)), (48, 48, (0, 3, 5, 8)), (96, 48, (0, 2, 5, 8))),
    ((0, 48, (0, 3, 6, 8)), (48, 32, (0, 3, 5, 8)), (80, 32, (0, 2, 5, 8))),
)
SET_LINKS = ((0, 2, 1), (2, 1, 0), (1, 0, 2))
MIB = 1 << 20
LANES = 128


def units(s, parts):
    found, offset = [], 0
    for part in parts:
        for row, count, cuts in THIRDS[part]:
            for unit in range(cuts[s], cuts[s + 1]):
                found.append((BEGINS[part] + row, count, unit, offset))
                offset += count
    return found, offset


def xor_shift(value):
    return value ^ lax.shift_right_logical(value, jnp.int32(16))


def mixing(value):
    value = xor_shift(value) * 73244475
    value = xor_shift(value) * 73244475
    return xor_shift(value)


def pack_body(k_hbm, v_hbm, out, k, sems):
    k_copy = pltpu.make_async_copy(k_hbm, k, sems.at[0])
    v_copy = pltpu.make_async_copy(v_hbm, out.at[1], sems.at[1])
    k_copy.start()
    v_copy.start()
    k_copy.wait()
    turned = k[...].T
    out[0, :HD] = turned[:, :128]
    out[0, HD:] = turned[:, 128:]
    v_copy.wait()


def pack(k, v):
    return pl.pallas_call(
        pack_body,
        out_shape=jax.ShapeDtypeStruct((2, ROWS, HD), jnp.bfloat16),
        in_specs=[pl.BlockSpec(memory_space=pltpu.HBM)] * 2,
        out_specs=pl.BlockSpec(memory_space=pltpu.VMEM),
        scratch_shapes=[pltpu.VMEM((ROWS, HD), jnp.bfloat16), pltpu.SemaphoreType.DMA((2,))],
        compiler_params=pltpu.CompilerParams(vmem_limit_bytes=1 * MIB),
        name="pack",
    )(in_hbm(k), in_hbm(v))


def in_hbm(array):
    return pltpu.with_memory_space_constraint(array, pltpu.HBM)


def row_low(starts, row):
    low = jnp.zeros_like(row)
    for v in range(1, 8):
        low = jnp.maximum(low, jnp.where(row >= starts[v], starts[v], 0))
    return low


def slot_flip(slot):
    return (slot & 1) ^ (3 * ((slot >> 1) & 1)) ^ (4 * (slot >> 2))


def prepare_body(seed_ref, docs_hbm, q_hbm, w_hbm, keep, query, weight, starts, docs, q, row_hash, sems):
    ctx = lax.axis_index("ctx")
    tp = lax.axis_index("tp")
    docs_copy = pltpu.make_async_copy(docs_hbm, docs, sems.at[8])
    docs_copy.start()
    q_copy = pltpu.make_async_copy(q_hbm, q, sems.at[9])
    q_copy.start()
    w_copies = []
    for slot in range(8):
        column = pl.multiple_of((tp ^ slot_flip(slot)) * COLUMNS, COLUMNS)
        w_copies.append(
            pltpu.make_async_copy(
                w_hbm.at[:, pl.ds(column, COLUMNS)], weight.at[slot], sems.at[slot]
            )
        )
        w_copies[-1].start()

    row0 = ctx * ROWS
    head0 = tp * GROUP
    seed = seed_ref[0]
    rows = row0 + lax.broadcasted_iota(jnp.int32, (ROWS, 128), 0)
    lanes = lax.broadcasted_iota(jnp.int32, (ROWS, 128), 1)
    for h in range(GROUP):
        head_hash = mixing(jnp.full((8, 128), seed * 7919 + head0 + h, jnp.int32))[:1]
        row_hash[h] = mixing(head_hash ^ (rows * 65537)) + lanes
    docs_copy.wait()
    starts[0] = 0
    for v in range(1, 8):
        starts[v] = jnp.sum((docs[...] < v).astype(jnp.int32))
    n = (row0 - (row_low(starts, row0) & -ROWS)) // ROWS

    def step(t, _):
        for u in range(STEP):
            start = row0 - (STEP * t + u) * ROWS
            used = STEP * t + u <= n

            @pl.when(used)
            def _():
                def head(h, _):
                    for begin, count in zip(BEGINS, SIZES):
                        for half in range(2):
                            value = row_hash[h, begin : begin + count] + (start + half * 128)
                            value = xor_shift(value) * 73244475
                            value = xor_shift(value) * 73244475
                            kept = (value ^ KEEP_FLIP) >= KEEP_BOUND
                            lane = u * ROWS + half * 128
                            place = pl.ds(GROUP * begin + h * count, count)
                            keep[t, place, lane : lane + 128] = jnp.where(
                                kept, jnp.float32(1), jnp.float32(0)
                            ).astype(jnp.bfloat16)
                    return 0

                lax.fori_loop(0, GROUP, head, 0)

            @pl.when(jnp.logical_not(used))
            def _():
                keep[t, :, u * ROWS : (u + 1) * ROWS] = jnp.zeros((GROUP * ROWS, ROWS), jnp.bfloat16)

        return 0

    lax.fori_loop(0, n // STEP + 1, step, 0)
    q_copy.wait()
    for begin, count in zip(BEGINS, SIZES):
        for h in range(GROUP):
            scaled = q[begin : begin + count, h * HD : (h + 1) * HD].astype(jnp.float32) * QUERY_SCALE
            high = scaled.astype(jnp.bfloat16)
            low = (scaled - high.astype(jnp.float32)).astype(jnp.bfloat16)
            place = slice(GROUP * begin + h * count, GROUP * begin + (h + 1) * count)
            query[place, :HD] = high
            query[place, HD:] = low
    for copy in w_copies:
        copy.wait()


def prepare(seed, docs, queries, weight):
    vmem = pl.BlockSpec(memory_space=pltpu.VMEM)
    hbm = pl.BlockSpec(memory_space=pltpu.HBM)
    smem = pl.BlockSpec(memory_space=pltpu.SMEM)
    return pl.pallas_call(
        prepare_body,
        out_shape=[
            jax.ShapeDtypeStruct((STEPS, GROUP * ROWS, STEP * ROWS), jnp.bfloat16),
            jax.ShapeDtypeStruct((GROUP * ROWS, 2 * HD), jnp.bfloat16),
            jax.ShapeDtypeStruct((8, GROUP * HD, COLUMNS), jnp.bfloat16),
            jax.ShapeDtypeStruct((8,), jnp.int32),
        ],
        in_specs=[smem, hbm, hbm, hbm],
        out_specs=[vmem, vmem, vmem, smem],
        scratch_shapes=[
            pltpu.VMEM((32, 128), jnp.int32),
            pltpu.VMEM((ROWS, GROUP * HD), jnp.bfloat16),
            pltpu.VMEM((GROUP, ROWS, 128), jnp.int32),
            pltpu.SemaphoreType.DMA((10,)),
        ],
        compiler_params=pltpu.CompilerParams(vmem_limit_bytes=4 * MIB),
        cost_estimate=pl.CostEstimate(
            flops=400_000_000, bytes_accessed=28 * MIB, transcendentals=0
        ),
        name="prepare",
    )(seed, docs, queries, weight)


def project_body(side, parts, mixed, weight, outs):
    placed = [units(s, parts)[0] for s in range(3)]
    for slot in range(8):
        bits = [[(slot >> k) & 1 for k in SET_LINKS[s]] for s in range(3)]
        sets = [s for s in range(3) if bits[s][0] == side]
        if not sets:
            continue
        columns = [unit for s in sets for _, _, unit, _ in placed[s]]
        low, high = min(columns), max(columns) + 1
        product = jnp.dot(
            mixed, weight[slot, :, low * LANES : high * LANES], preferred_element_type=jnp.float32
        ).astype(jnp.bfloat16)
        for s in sets:
            at = 2 * bits[s][1] + bits[s][2]
            for row, count, unit, offset in placed[s]:
                row, lane = row - BEGINS[parts[0]], (unit - low) * LANES
                outs[s][at, offset : offset + count] = product[
                    row : row + count, lane : lane + LANES
                ]


def slots(count, parts):
    return [jax.ShapeDtypeStruct((count, units(s, parts)[1], LANES), jnp.bfloat16) for s in range(3)]


def rest_body(first, second, weight, *outs):
    mixed = jnp.concatenate([first[...], second[...]], axis=0)
    project_body(0, (0, 1), mixed, weight, outs)


def project_rest(first, second, weight):
    vmem = pl.BlockSpec(memory_space=pltpu.VMEM)
    return pl.pallas_call(
        rest_body,
        out_shape=slots(4, (0, 1)),
        in_specs=[vmem] * 3,
        out_specs=[vmem] * 3,
        compiler_params=pltpu.CompilerParams(vmem_limit_bytes=6 * MIB),
        cost_estimate=pl.CostEstimate(
            flops=2_100_000_000, bytes_accessed=4 * MIB, transcendentals=0
        ),
        name="rest",
    )(first, second, weight)


def turn_body(n, own, other, keys, values):
    core = lax.axis_index("ctx") & 1

    def place(d):
        t, lane = d // STEP, d % STEP * ROWS
        source, at = (other, (d + 1) // 2 - core) if d % 2 else (own, d // 2)
        for half in range(2):
            turned = source[at, 0, half * HD : (half + 1) * HD]
            at_lane = slice(lane + half * 128, lane + (half + 1) * 128)
            keys[t, :HD, at_lane] = turned
            keys[t, HD:, at_lane] = turned
        values[t, lane : lane + ROWS] = source[at, 1]

    for t in range(STEPS):

        @pl.when(STEP * t <= n)
        def _():
            for d in range(STEP * t, STEP * (t + 1)):
                place(d)


def attend_body(part, starts, query, *refs):
    if part:
        keys, values, keep, weight, mixed, *refs = refs
    else:
        own, other, keep, weight, keys, values, mixed, *refs = refs
    sends = refs[:3]
    score, peak, total, accum, bias = refs[3:]
    block0 = lax.axis_index("ctx") * ROWS
    n = (block0 - (row_low(starts, block0) & -ROWS)) // ROWS
    if not part:
        turn_body(n, own, other, keys, values)
    rows = SIZES[part]
    row0 = block0 + BEGINS[part]
    span = slice(GROUP * BEGINS[part], GROUP * (BEGINS[part] + rows))
    last_low = row_low(starts, row0 + rows - 1)
    peak[...] = jnp.full(peak.shape, -3e38, jnp.float32)
    total[...] = jnp.zeros(total.shape, jnp.float32)
    accum[...] = jnp.zeros(accum.shape, jnp.float32)

    def score_step(t, masked):
        value = jnp.dot(query[span], keys[t], preferred_element_type=jnp.float32)
        if masked:
            lane = lax.broadcasted_iota(jnp.int32, (rows, STEP * ROWS), 1)
            key_pos = block0 - STEP * t * ROWS - (lane & -ROWS) + (lane & (ROWS - 1))
            row_pos = row0 + lax.broadcasted_iota(jnp.int32, (rows, 1), 0)
            allowed = (key_pos >= row_low(starts, row_pos)) & (key_pos <= row_pos)
            bias[...] = jnp.where(allowed, jnp.float32(0), jnp.float32(-1e30))
            value = value.reshape(GROUP, rows, STEP * ROWS) + bias[...][None]
            value = value.reshape(GROUP * rows, STEP * ROWS)
        score[t] = value
        top = peak[...]
        for k in range(STEP * ROWS // 128):
            top = jnp.maximum(top, value[:, k * 128 : (k + 1) * 128])
        peak[...] = top

    def score_loop(t, _):
        free = (t > 0) & (block0 - (STEP * t + STEP - 1) * ROWS >= last_low)

        @pl.when(free)
        def _():
            score_step(t, False)

        @pl.when(jnp.logical_not(free))
        def _():
            score_step(t, True)

        return 0

    lax.fori_loop(0, n // STEP + 1, score_loop, 0)
    peak[...] = jnp.broadcast_to(jnp.max(peak[...], axis=1, keepdims=True), peak.shape)

    def value_loop(t, _):
        top = peak[...]
        added = total[...]
        probs = []
        for k in range(STEP * ROWS // 128):
            prob = jnp.exp2(score[t, :, k * 128 : (k + 1) * 128] - top)
            added = added + prob
            probs.append(prob.astype(jnp.bfloat16))
        total[...] = added
        prob = jnp.concatenate(probs, axis=1) * keep[t, span]
        accum[...] = accum[...] + jnp.dot(prob, values[t], preferred_element_type=jnp.float32)
        return 0

    lax.fori_loop(0, n // STEP + 1, value_loop, 0)
    for h in range(GROUP):
        at = slice(h * rows, (h + 1) * rows)
        row_sum = jnp.sum(total[at], axis=1, keepdims=True) * 0.9
        mixed[:, h * HD : (h + 1) * HD] = (accum[at] / row_sum).astype(jnp.bfloat16)

    project_body(1, (part,), mixed[...], weight, sends)


def attend(part, starts, query, sources, keep, weight):
    vmem = pl.BlockSpec(memory_space=pltpu.VMEM)
    rows = SIZES[part]
    heads_rows = GROUP * rows
    out_shape = [
        jax.ShapeDtypeStruct((STEPS, 2 * HD, STEP * ROWS), jnp.bfloat16),
        jax.ShapeDtypeStruct((STEPS, STEP * ROWS, HD), jnp.bfloat16),
        jax.ShapeDtypeStruct((rows, GROUP * HD), jnp.bfloat16),
    ] + slots(4, (part,))
    out_shape = out_shape[2 if part else 0 :]
    return pl.pallas_call(
        functools.partial(attend_body, part),
        out_shape=out_shape,
        in_specs=[pl.BlockSpec(memory_space=pltpu.SMEM)] + [vmem] * 5,
        out_specs=[vmem] * len(out_shape),
        scratch_shapes=[
            pltpu.VMEM((STEPS, heads_rows, STEP * ROWS), jnp.float32),
            pltpu.VMEM((heads_rows, 128), jnp.float32),
            pltpu.VMEM((heads_rows, 128), jnp.float32),
            pltpu.VMEM((heads_rows, HD), jnp.float32),
            pltpu.VMEM((rows, STEP * ROWS), jnp.float32),
        ],
        compiler_params=pltpu.CompilerParams(vmem_limit_bytes=16 * MIB),
        cost_estimate=pl.CostEstimate(
            flops=3_000_000_000, bytes_accessed=16 * MIB, transcendentals=3_000_000
        ),
        name=f"attend_{part}",
    )(starts, query, *sources, keep, weight)


def fold_body(count, *refs):
    rest, got, (kept, sent) = refs[0], refs[1:-2], refs[-2:]
    offset = 0
    for other in got:
        rows = other.shape[1]
        for j in range(count):
            held = rest[j, offset : offset + rows].astype(jnp.float32) + other[j].astype(jnp.float32)
            target = kept if j < count // 2 else sent
            target[j % (count // 2), offset : offset + rows] = held.astype(jnp.bfloat16)
        offset += rows


def fold(rest, got):
    vmem = pl.BlockSpec(memory_space=pltpu.VMEM)
    count = rest.shape[0]
    half = jax.ShapeDtypeStruct((count // 2,) + rest.shape[1:], jnp.bfloat16)
    return pl.pallas_call(
        functools.partial(fold_body, count),
        out_shape=[half] * 2,
        in_specs=[vmem] * (1 + len(got)),
        out_specs=[vmem] * 2,
        compiler_params=pltpu.CompilerParams(vmem_limit_bytes=2 * MIB),
        cost_estimate=pl.CostEstimate(flops=300_000, bytes_accessed=MIB, transcendentals=0),
        name=f"fold_{count}",
    )(rest, *got)


def finish_body(*refs):
    out = refs[6]
    for s in range(3):
        for row, count, unit, offset in units(s, (0, 1))[0]:
            held = refs[2 * s][0, offset : offset + count].astype(jnp.float32)
            held = held + refs[2 * s + 1][0, offset : offset + count].astype(jnp.float32)
            out[row : row + count, unit * LANES : (unit + 1) * LANES] = held.astype(jnp.bfloat16)


def finish(pairs):
    vmem = pl.BlockSpec(memory_space=pltpu.VMEM)
    return pl.pallas_call(
        finish_body,
        out_shape=jax.ShapeDtypeStruct((ROWS, COLUMNS), jnp.bfloat16),
        in_specs=[vmem] * 6,
        out_specs=vmem,
        compiler_params=pltpu.CompilerParams(vmem_limit_bytes=4 * MIB),
        name="finish",
    )(*pairs)


def swap(array, flip):
    return lax.ppermute(array, "tp", [(i, i ^ flip) for i in range(8)])


def after(first, second):
    return lax.optimization_barrier((first, second))


def body(queries, key_proj, value_proj, out_weight, doc_ids, drop_seed):
    own = pack(key_proj, value_proj)
    column = [own] * 5
    for chips in (2, 4, 1, 3):
        pairs = [(i, (i + 2 * chips) % 16) for i in range(16)]
        column[chips] = lax.ppermute(own, "ctx", pairs)
    column = jnp.stack(column)
    keep, query, weight, starts = prepare(
        drop_seed, in_hbm(doc_ids.reshape(32, 128)), in_hbm(queries), in_hbm(out_weight)
    )
    column, keep = after(column, keep)
    other = lax.ppermute(column, "ctx", [(i, i ^ 1) for i in range(16)])

    keys, values, first, *sent = attend(0, starts, query, (column, other), keep, weight)
    keep, sent = after(keep, sent)
    got = [[swap(sent[s], LINK_FLIPS[SET_LINKS[s][0]])] for s in range(3)]
    second, *sent = attend(1, starts, query, (keys, values), keep, weight)
    second, sent = after(second, sent)
    for s in range(3):
        sent[s], got[s] = after(sent[s], got[s])
        got[s].append(swap(sent[s], LINK_FLIPS[SET_LINKS[s][0]]))
    rest = list(project_rest(first, second, weight))
    order = second
    for step in (1, 2):
        for s in range(3):
            rest[s], got[s], order = lax.optimization_barrier((rest[s], got[s], order))
            rest[s], order = fold(rest[s], got[s])
            got[s] = [swap(order, LINK_FLIPS[SET_LINKS[s][step]])]
    return finish([array for s in range(3) for array in (rest[s], got[s][0])])


def solution(mesh):
    in_specs = (P("ctx", "tp"), P("ctx", "tp"), P("ctx", "tp"), P("tp", None), P(), P())
    return jax.shard_map(
        body, mesh=mesh, in_specs=in_specs, out_specs=P("ctx", "tp"), check_vma=False
    )
```

```python
import functools
import math

import jax
import jax.numpy as jnp
from jax import lax
from jax.experimental import pallas as pl
from jax.experimental.pallas import tpu as pltpu
from jax.sharding import PartitionSpec as P

HEADS = 64
KVH = 8
HD = 128
GROUP = HEADS // KVH
ROWS = 256
BACK = 8
STEP = 3
STEPS = (BACK + STEP) // STEP
QUERY_SCALE = HD ** (-0.5) * math.log2(math.e)
INT_MIN = -(1 << 31)
KEEP_FLIP = 0x1999 + INT_MIN
KEEP_BOUND = (1677722 << 8) + INT_MIN
COLUMNS = 1024
LINK_FLIPS = (1, 3, 4)
SIZES = (144, 112)
BEGINS = (0, 144)
THIRDS = (
    ((0, 48, (0, 3, 6, 8)), (48, 48, (0, 3, 5, 8)), (96, 48, (0, 2, 5, 8))),
    ((0, 48, (0, 3, 6, 8)), (48, 32, (0, 3, 5, 8)), (80, 32, (0, 2, 5, 8))),
)
SET_LINKS = ((0, 2, 1), (2, 1, 0), (1, 0, 2))
MIB = 1 << 20
LANES = 128


def units(s, parts):
    found, offset = [], 0
    for part in parts:
        for row, count, cuts in THIRDS[part]:
            for unit in range(cuts[s], cuts[s + 1]):
                found.append((BEGINS[part] + row, count, unit, offset))
                offset += count
    return found, offset


def xor_shift(value):
    return value ^ lax.shift_right_logical(value, jnp.int32(16))


def mixing(value):
    value = xor_shift(value) * 73244475
    value = xor_shift(value) * 73244475
    return xor_shift(value)


def pack_body(k_hbm, v_hbm, out, k, sems):
    k_copy = pltpu.make_async_copy(k_hbm, k, sems.at[0])
    v_copy = pltpu.make_async_copy(v_hbm, out.at[1], sems.at[1])
    k_copy.start()
    v_copy.start()
    k_copy.wait()
    turned = k[...].T
    out[0, :HD] = turned[:, :128]
    out[0, HD:] = turned[:, 128:]
    v_copy.wait()


def pack(k, v):
    return pl.pallas_call(
        pack_body,
        out_shape=jax.ShapeDtypeStruct((2, ROWS, HD), jnp.bfloat16),
        in_specs=[pl.BlockSpec(memory_space=pltpu.HBM)] * 2,
        out_specs=pl.BlockSpec(memory_space=pltpu.VMEM),
        scratch_shapes=[pltpu.VMEM((ROWS, HD), jnp.bfloat16), pltpu.SemaphoreType.DMA((2,))],
        compiler_params=pltpu.CompilerParams(vmem_limit_bytes=1 * MIB),
        name="pack",
    )(in_hbm(k), in_hbm(v))


def in_hbm(array):
    return pltpu.with_memory_space_constraint(array, pltpu.HBM)


def row_low(starts, row):
    low = jnp.zeros_like(row)
    for v in range(1, 8):
        low = jnp.maximum(low, jnp.where(row >= starts[v], starts[v], 0))
    return low


def slot_flip(slot):
    return (slot & 1) ^ (3 * ((slot >> 1) & 1)) ^ (4 * (slot >> 2))


def prepare_body(seed_ref, docs_hbm, q_hbm, w_hbm, keep, query, weight, starts, docs, q, row_hash, sems):
    ctx = lax.axis_index("ctx")
    tp = lax.axis_index("tp")
    docs_copy = pltpu.make_async_copy(docs_hbm, docs, sems.at[8])
    docs_copy.start()
    q_copy = pltpu.make_async_copy(q_hbm, q, sems.at[9])
    q_copy.start()
    w_copies = []
    for slot in range(8):
        column = pl.multiple_of((tp ^ slot_flip(slot)) * COLUMNS, COLUMNS)
        w_copies.append(
            pltpu.make_async_copy(
                w_hbm.at[:, pl.ds(column, COLUMNS)], weight.at[slot], sems.at[slot]
            )
        )
        w_copies[-1].start()

    row0 = ctx * ROWS
    head0 = tp * GROUP
    seed = seed_ref[0]
    rows = row0 + lax.broadcasted_iota(jnp.int32, (ROWS, 128), 0)
    lanes = lax.broadcasted_iota(jnp.int32, (ROWS, 128), 1)
    for h in range(GROUP):
        head_hash = mixing(jnp.full((8, 128), seed * 7919 + head0 + h, jnp.int32))[:1]
        row_hash[h] = mixing(head_hash ^ (rows * 65537)) + lanes
    docs_copy.wait()
    starts[0] = 0
    for v in range(1, 8):
        starts[v] = jnp.sum((docs[...] < v).astype(jnp.int32))
    n = (row0 - (row_low(starts, row0) & -ROWS)) // ROWS

    def step(t, _):
        for u in range(STEP):
            start = row0 - (STEP * t + u) * ROWS
            used = STEP * t + u <= n

            @pl.when(used)
            def _():
                def head(h, _):
                    for begin, count in zip(BEGINS, SIZES):
                        for half in range(2):
                            value = row_hash[h, begin : begin + count] + (start + half * 128)
                            value = xor_shift(value) * 73244475
                            value = xor_shift(value) * 73244475
                            kept = (value ^ KEEP_FLIP) >= KEEP_BOUND
                            lane = u * ROWS + half * 128
                            place = pl.ds(GROUP * begin + h * count, count)
                            keep[t, place, lane : lane + 128] = jnp.where(
                                kept, jnp.float32(1), jnp.float32(0)
                            ).astype(jnp.bfloat16)
                    return 0

                lax.fori_loop(0, GROUP, head, 0)

            @pl.when(jnp.logical_not(used))
            def _():
                keep[t, :, u * ROWS : (u + 1) * ROWS] = jnp.zeros((GROUP * ROWS, ROWS), jnp.bfloat16)

        return 0

    lax.fori_loop(0, n // STEP + 1, step, 0)
    q_copy.wait()
    for begin, count in zip(BEGINS, SIZES):
        for h in range(GROUP):
            scaled = q[begin : begin + count, h * HD : (h + 1) * HD].astype(jnp.float32) * QUERY_SCALE
            high = scaled.astype(jnp.bfloat16)
            low = (scaled - high.astype(jnp.float32)).astype(jnp.bfloat16)
            place = slice(GROUP * begin + h * count, GROUP * begin + (h + 1) * count)
            query[place, :HD] = high
            query[place, HD:] = low
    for copy in w_copies:
        copy.wait()


def prepare(seed, docs, queries, weight):
    vmem = pl.BlockSpec(memory_space=pltpu.VMEM)
    hbm = pl.BlockSpec(memory_space=pltpu.HBM)
    smem = pl.BlockSpec(memory_space=pltpu.SMEM)
    return pl.pallas_call(
        prepare_body,
        out_shape=[
            jax.ShapeDtypeStruct((STEPS, GROUP * ROWS, STEP * ROWS), jnp.bfloat16),
            jax.ShapeDtypeStruct((GROUP * ROWS, 2 * HD), jnp.bfloat16),
            jax.ShapeDtypeStruct((8, GROUP * HD, COLUMNS), jnp.bfloat16),
            jax.ShapeDtypeStruct((8,), jnp.int32),
        ],
        in_specs=[smem, hbm, hbm, hbm],
        out_specs=[vmem, vmem, vmem, smem],
        scratch_shapes=[
            pltpu.VMEM((32, 128), jnp.int32),
            pltpu.VMEM((ROWS, GROUP * HD), jnp.bfloat16),
            pltpu.VMEM((GROUP, ROWS, 128), jnp.int32),
            pltpu.SemaphoreType.DMA((10,)),
        ],
        compiler_params=pltpu.CompilerParams(vmem_limit_bytes=4 * MIB),
        cost_estimate=pl.CostEstimate(
            flops=400_000_000, bytes_accessed=28 * MIB, transcendentals=0
        ),
        name="prepare",
    )(seed, docs, queries, weight)


def project_body(side, parts, mixed, weight, outs):
    placed = [units(s, parts)[0] for s in range(3)]
    for slot in range(8):
        bits = [[(slot >> k) & 1 for k in SET_LINKS[s]] for s in range(3)]
        sets = [s for s in range(3) if bits[s][0] == side]
        if not sets:
            continue
        columns = [unit for s in sets for _, _, unit, _ in placed[s]]
        low, high = min(columns), max(columns) + 1
        product = jnp.dot(
            mixed, weight[slot, :, low * LANES : high * LANES], preferred_element_type=jnp.float32
        ).astype(jnp.bfloat16)
        for s in sets:
            at = 2 * bits[s][1] + bits[s][2]
            for row, count, unit, offset in placed[s]:
                row, lane = row - BEGINS[parts[0]], (unit - low) * LANES
                outs[s][at, offset : offset + count] = product[
                    row : row + count, lane : lane + LANES
                ]


def slots(count, parts):
    return [jax.ShapeDtypeStruct((count, units(s, parts)[1], LANES), jnp.bfloat16) for s in range(3)]


def rest_body(first, second, weight, *outs):
    mixed = jnp.concatenate([first[...], second[...]], axis=0)
    project_body(0, (0, 1), mixed, weight, outs)


def project_rest(first, second, weight):
    vmem = pl.BlockSpec(memory_space=pltpu.VMEM)
    return pl.pallas_call(
        rest_body,
        out_shape=slots(4, (0, 1)),
        in_specs=[vmem] * 3,
        out_specs=[vmem] * 3,
        compiler_params=pltpu.CompilerParams(vmem_limit_bytes=6 * MIB),
        cost_estimate=pl.CostEstimate(
            flops=2_100_000_000, bytes_accessed=4 * MIB, transcendentals=0
        ),
        name="rest",
    )(first, second, weight)


def turn_body(n, own, other, keys, values):
    core = lax.axis_index("ctx") & 1

    def place(d):
        t, lane = d // STEP, d % STEP * ROWS
        source, at = (other, (d + 1) // 2 - core) if d % 2 else (own, d // 2)
        for half in range(2):
            turned = source[at, 0, half * HD : (half + 1) * HD]
            at_lane = slice(lane + half * 128, lane + (half + 1) * 128)
            keys[t, :HD, at_lane] = turned
            keys[t, HD:, at_lane] = turned
        values[t, lane : lane + ROWS] = source[at, 1]

    for t in range(STEPS):

        @pl.when(STEP * t <= n)
        def _():
            for d in range(STEP * t, STEP * (t + 1)):
                place(d)


def attend_body(part, starts, query, *refs):
    if part:
        keys, values, keep, weight, mixed, *refs = refs
    else:
        own, other, keep, weight, keys, values, mixed, *refs = refs
    sends = refs[:3]
    score, peak, total, accum, bias = refs[3:]
    block0 = lax.axis_index("ctx") * ROWS
    n = (block0 - (row_low(starts, block0) & -ROWS)) // ROWS
    if not part:
        turn_body(n, own, other, keys, values)
    rows = SIZES[part]
    row0 = block0 + BEGINS[part]
    span = slice(GROUP * BEGINS[part], GROUP * (BEGINS[part] + rows))
    last_low = row_low(starts, row0 + rows - 1)
    peak[...] = jnp.full(peak.shape, -3e38, jnp.float32)
    total[...] = jnp.zeros(total.shape, jnp.float32)
    accum[...] = jnp.zeros(accum.shape, jnp.float32)

    def score_step(t, masked):
        value = jnp.dot(query[span], keys[t], preferred_element_type=jnp.float32)
        if masked:
            lane = lax.broadcasted_iota(jnp.int32, (rows, STEP * ROWS), 1)
            key_pos = block0 - STEP * t * ROWS - (lane & -ROWS) + (lane & (ROWS - 1))
            row_pos = row0 + lax.broadcasted_iota(jnp.int32, (rows, 1), 0)
            allowed = (key_pos >= row_low(starts, row_pos)) & (key_pos <= row_pos)
            bias[...] = jnp.where(allowed, jnp.float32(0), jnp.float32(-1e30))
            value = value.reshape(GROUP, rows, STEP * ROWS) + bias[...][None]
            value = value.reshape(GROUP * rows, STEP * ROWS)
        score[t] = value
        top = peak[...]
        for k in range(STEP * ROWS // 128):
            top = jnp.maximum(top, value[:, k * 128 : (k + 1) * 128])
        peak[...] = top

    def score_loop(t, _):
        free = (t > 0) & (block0 - (STEP * t + STEP - 1) * ROWS >= last_low)

        @pl.when(free)
        def _():
            score_step(t, False)

        @pl.when(jnp.logical_not(free))
        def _():
            score_step(t, True)

        return 0

    lax.fori_loop(0, n // STEP + 1, score_loop, 0)
    peak[...] = jnp.broadcast_to(jnp.max(peak[...], axis=1, keepdims=True), peak.shape)

    def value_loop(t, _):
        top = peak[...]
        added = total[...]
        probs = []
        for k in range(STEP * ROWS // 128):
            prob = jnp.exp2(score[t, :, k * 128 : (k + 1) * 128] - top)
            added = added + prob
            probs.append(prob.astype(jnp.bfloat16))
        total[...] = added
        prob = jnp.concatenate(probs, axis=1) * keep[t, span]
        accum[...] = accum[...] + jnp.dot(prob, values[t], preferred_element_type=jnp.float32)
        return 0

    lax.fori_loop(0, n // STEP + 1, value_loop, 0)
    for h in range(GROUP):
        at = slice(h * rows, (h + 1) * rows)
        row_sum = jnp.sum(total[at], axis=1, keepdims=True) * 0.9
        mixed[:, h * HD : (h + 1) * HD] = (accum[at] / row_sum).astype(jnp.bfloat16)

    project_body(1, (part,), mixed[...], weight, sends)


def attend(part, starts, query, sources, keep, weight):
    vmem = pl.BlockSpec(memory_space=pltpu.VMEM)
    rows = SIZES[part]
    heads_rows = GROUP * rows
    out_shape = [
        jax.ShapeDtypeStruct((STEPS, 2 * HD, STEP * ROWS), jnp.bfloat16),
        jax.ShapeDtypeStruct((STEPS, STEP * ROWS, HD), jnp.bfloat16),
        jax.ShapeDtypeStruct((rows, GROUP * HD), jnp.bfloat16),
    ] + slots(4, (part,))
    out_shape = out_shape[2 if part else 0 :]
    return pl.pallas_call(
        functools.partial(attend_body, part),
        out_shape=out_shape,
        in_specs=[pl.BlockSpec(memory_space=pltpu.SMEM)] + [vmem] * 5,
        out_specs=[vmem] * len(out_shape),
        scratch_shapes=[
            pltpu.VMEM((STEPS, heads_rows, STEP * ROWS), jnp.float32),
            pltpu.VMEM((heads_rows, 128), jnp.float32),
            pltpu.VMEM((heads_rows, 128), jnp.float32),
            pltpu.VMEM((heads_rows, HD), jnp.float32),
            pltpu.VMEM((rows, STEP * ROWS), jnp.float32),
        ],
        compiler_params=pltpu.CompilerParams(vmem_limit_bytes=16 * MIB),
        cost_estimate=pl.CostEstimate(
            flops=3_000_000_000, bytes_accessed=16 * MIB, transcendentals=3_000_000
        ),
        name=f"attend_{part}",
    )(starts, query, *sources, keep, weight)


def fold_body(count, *refs):
    rest, got, (kept, sent) = refs[0], refs[1:-2], refs[-2:]
    offset = 0
    for other in got:
        rows = other.shape[1]
        for j in range(count):
            held = rest[j, offset : offset + rows].astype(jnp.float32) + other[j].astype(jnp.float32)
            target = kept if j < count // 2 else sent
            target[j % (count // 2), offset : offset + rows] = held.astype(jnp.bfloat16)
        offset += rows


def fold(rest, got):
    vmem = pl.BlockSpec(memory_space=pltpu.VMEM)
    count = rest.shape[0]
    half = jax.ShapeDtypeStruct((count // 2,) + rest.shape[1:], jnp.bfloat16)
    return pl.pallas_call(
        functools.partial(fold_body, count),
        out_shape=[half] * 2,
        in_specs=[vmem] * (1 + len(got)),
        out_specs=[vmem] * 2,
        compiler_params=pltpu.CompilerParams(vmem_limit_bytes=2 * MIB),
        cost_estimate=pl.CostEstimate(flops=300_000, bytes_accessed=MIB, transcendentals=0),
        name=f"fold_{count}",
    )(rest, *got)


def finish_body(sets, *refs):
    pairs = refs[: 2 * len(sets)]
    out, held, sems = refs[-3:]
    copies = []
    for part in range(2):
        for row, count, cuts in THIRDS[part]:
            row += BEGINS[part]
            for index, s in enumerate(sets):
                for place, _, unit, offset in units(s, (0, 1))[0]:
                    if place != row:
                        continue
                    total = pairs[2 * index][0, offset : offset + count].astype(jnp.float32)
                    total = total + pairs[2 * index + 1][0, offset : offset + count].astype(jnp.float32)
                    held[row : row + count, unit * LANES : (unit + 1) * LANES] = total.astype(jnp.bfloat16)
            columns = slice(cuts[sets[0]] * LANES, cuts[sets[-1] + 1] * LANES)
            copies.append(
                pltpu.make_async_copy(
                    held.at[row : row + count, columns],
                    out.at[row : row + count, columns],
                    sems.at[len(copies)],
                )
            )
            copies[-1].start()
    for copy in copies:
        copy.wait()


def finish(sets, pairs, before):
    vmem = pl.BlockSpec(memory_space=pltpu.VMEM)
    hbm = pl.BlockSpec(memory_space=pltpu.HBM)
    old = [] if before is None else [before]
    return pl.pallas_call(
        functools.partial(finish_body, sets),
        out_shape=jax.ShapeDtypeStruct((ROWS, COLUMNS), jnp.bfloat16),
        in_specs=[vmem] * len(pairs) + [hbm] * len(old),
        out_specs=hbm,
        input_output_aliases={len(pairs): 0} if old else {},
        scratch_shapes=[pltpu.VMEM((ROWS, COLUMNS), jnp.bfloat16), pltpu.SemaphoreType.DMA((6,))],
        compiler_params=pltpu.CompilerParams(vmem_limit_bytes=4 * MIB),
        cost_estimate=pl.CostEstimate(flops=300_000, bytes_accessed=MIB, transcendentals=0),
        name=f"finish_{sets[0]}",
    )(*pairs, *old)


def swap(array, flip):
    return lax.ppermute(array, "tp", [(i, i ^ flip) for i in range(8)])


def after(first, second):
    return lax.optimization_barrier((first, second))


def body(queries, key_proj, value_proj, out_weight, doc_ids, drop_seed):
    own = pack(key_proj, value_proj)
    column = [own] * 5
    for chips in (2, 4, 1, 3):
        pairs = [(i, (i + 2 * chips) % 16) for i in range(16)]
        column[chips] = lax.ppermute(own, "ctx", pairs)
    column = jnp.stack(column)
    keep, query, weight, starts = prepare(
        drop_seed, in_hbm(doc_ids.reshape(32, 128)), in_hbm(queries), in_hbm(out_weight)
    )
    column, keep = after(column, keep)
    other = lax.ppermute(column, "ctx", [(i, i ^ 1) for i in range(16)])

    keys, values, first, *sent = attend(0, starts, query, (column, other), keep, weight)
    keep, sent = after(keep, sent)
    got = [[swap(sent[s], LINK_FLIPS[SET_LINKS[s][0]])] for s in range(3)]
    second, *sent = attend(1, starts, query, (keys, values), keep, weight)
    second, sent = after(second, sent)
    for s in range(3):
        sent[s], got[s] = after(sent[s], got[s])
        got[s].append(swap(sent[s], LINK_FLIPS[SET_LINKS[s][0]]))
    rest = list(project_rest(first, second, weight))
    order = second
    for step in (1, 2):
        for s in range(3):
            rest[s], got[s], order = lax.optimization_barrier((rest[s], got[s], order))
            rest[s], order = fold(rest[s], got[s])
            got[s] = [swap(order, LINK_FLIPS[SET_LINKS[s][step]])]
    pairs = [(rest[s], got[s][0]) for s in range(3)]
    result = finish((0, 1), pairs[0] + pairs[1], None)
    return finish((2,), pairs[2], result)


def solution(mesh):
    in_specs = (P("ctx", "tp"), P("ctx", "tp"), P("ctx", "tp"), P("tp", None), P(), P())
    return jax.shard_map(
        body, mesh=mesh, in_specs=in_specs, out_specs=P("ctx", "tp"), check_vma=False
    )
```
